256 devices in a mesh: depth: 8 (over y_lo, x), gx: 32 (over z, y_hi, core).
Axes of the slice: x: 4, y: 4 (y_hi: 2, y_lo: 2; y = y_hi * 2 + y_lo), z: 8, core: 2. Of those that a mesh axis runs over, the one named last changes fastest.
Arguments:
- offset_image: bfloat16 [64, 128, 128, 256], P(None, 'depth', 'gx'), may hold values from -6 to 6
- dip_class: int32 [128, 128, 256], P('depth', 'gx'), may hold values from 0 to 7
- slant_taper: bfloat16 [64, 64, 33], replicated, may hold values from -0.3125 to 0.3125
- band_offsets: int32 [64], replicated, may hold values from -14 to 14
- coefficients: float32 [8, 27], replicated, may hold values from -1.25 to 1.25
Outputs:
- smoothed: bfloat16 [64, 128, 128, 256], P(None, 'depth', 'gx')
The draws below stay inside these ranges and needn't reach their ends.
All inputs are finite; a program needn't handle non-finite values.
Results may differ from the reference program's by a relative error of at most 0.0049.
Values may be sent and summed in bfloat16 or wider, within the bound.
No kernel may reach another device: no remote copies, remote signals or barrier semaphores. Data moves between devices by JAX's collectives and lax.ppermute only.
A program may use at most 64 MiB of HBM per device.

```python
import jax
import jax.numpy as jnp
from jax import lax

H = 64
ANG = 64
R = 16
BAND = 2
RX = 4
RY = 1
NQ = 8
NY = 256
TAPS = 27
NZ = 128
NX = 128


def place_ends(array, rng, low, largest):
    extent = array.shape
    spot = [jax.random.randint(jax.random.fold_in(rng, axis), (), 0, extent[axis]) for axis in range(len(extent))]
    array = array.at[tuple(spot)].set(low)
    longest = extent.index(max(extent))
    spot[longest] = (spot[longest] + 1) % extent[longest]
    return array.at[tuple(spot)].set(largest)


def levels(own_key, extent, cuts, low, top_value):
    factor_of = 1.0
    for dim, blocks in cuts:
        draws = jax.random.uniform(jax.random.fold_in(jax.random.fold_in(own_key, 6), dim), (blocks,), jnp.float32, low / len(cuts), top_value / len(cuts))
        factor_of = factor_of * jnp.repeat(jnp.exp(draws), extent[dim] // blocks).reshape((-1,) + (1,) * (len(extent) - 1 - dim))
    return factor_of


def bell_draw(key, shape, spread, reach, shards=(), kind=jnp.bfloat16):
    array = jax.random.normal(key, shape, jnp.float32) * spread
    if len(shards) > 0:
        array = levels(key, shape, shards, -0.22, 0.18) * array
    return jnp.clip(array, min=-reach, max=reach).astype(kind)


def setup_inputs(seed: int = 0) -> dict:
    arg_keys = jax.random.split(jax.random.key(seed), 6)
    return {
        "offset_image": bell_draw(arg_keys[0], (H, NZ, NX, NY), 1.0, 6.0, ((1, 8), (2, 32))),
        "dip_class": place_ends(jax.random.randint(arg_keys[1], (NZ, NX, NY), 0, NQ), jax.random.fold_in(arg_keys[1], 1), 0, NQ - 1).astype(jnp.int32),
        "slant_taper": bell_draw(arg_keys[2], (ANG, H, 2 * R + 1), (H * (2 * BAND + 1)) ** -0.5, 0.3125),
        "band_offsets": place_ends(jax.random.randint(arg_keys[3], (ANG,), BAND - R, R - BAND + 1), jax.random.fold_in(arg_keys[3], 1), BAND - R, R - BAND).astype(jnp.int32),
        "coefficients": bell_draw(arg_keys[4], (NQ, TAPS), TAPS ** -0.5, 1.25, (), jnp.float32),
    }


def slant_matrix_of(slant_taper, band_offsets, offset_count):
    offset_index = jnp.arange(offset_count, dtype=jnp.int32)
    depth_shift = jnp.floor_divide(band_offsets[:, None] * offset_index[None, :], offset_count)
    reach_index = jnp.arange(slant_taper.shape[2], dtype=jnp.int32) - R
    inside_band = jnp.abs(reach_index[None, None, :] - depth_shift[:, :, None]) <= BAND
    return jnp.where(inside_band, slant_taper, jnp.zeros_like(slant_taper))


def reference(offset_image, dip_class, slant_taper, band_offsets, coefficients):
    slant_matrix = slant_matrix_of(slant_taper, band_offsets, H).astype(jnp.float32)
    padded = jnp.pad(offset_image, ((0, 0), (R, R), (0, 0), (0, 0)))

    def one_depth(depth_level):
        window = lax.dynamic_slice_in_dim(padded, depth_level, 2 * R + 1, 1).astype(jnp.float32)
        return jnp.einsum("ahd,hdxy->axy", slant_matrix, window).astype(jnp.bfloat16)

    gathers = jnp.moveaxis(lax.map(one_depth, jnp.arange(NZ, dtype=jnp.int32)), 0, 1)
    tap_weights = jnp.moveaxis(jnp.take(coefficients, dip_class, axis=0), 3, 0)
    widened = jnp.pad(gathers, ((0, 0), (0, 0), (RX, RX), (RY, RY)))

    def smooth_angle(angle_plane):
        running = jnp.zeros((NZ, NX, NY), jnp.float32)
        for column_step in range(2 * RX + 1):
            for row_step in range(2 * RY + 1):
                tap_index = column_step * (2 * RY + 1) + row_step
                shifted = angle_plane[:, column_step:column_step + NX, row_step:row_step + NY]
                running = running + tap_weights[tap_index] * shifted.astype(jnp.float32)
        return running.astype(jnp.bfloat16)

    return lax.map(smooth_angle, widened)
```

```python
import functools

import jax
import jax.numpy as jnp
from jax import lax
from jax.experimental import pallas as pl
from jax.experimental.pallas import tpu as pltpu
from jax.sharding import PartitionSpec as P

R = 16
BAND = 2
RX = 4
RY = 1
REACH = R - BAND
ZB = 4
BF = jnp.bfloat16
F32 = jnp.float32


def reach_tables(offsets, steps):
    before, after = [], []
    for k in range(1, steps + 1):
        low = [h for h in range(offsets) if -((-REACH * h) // offsets) + BAND >= k]
        high = [h for h in range(offsets) if (REACH * h) // offsets + BAND >= k]
        if low:
            before.append(low[0])
        if high:
            after.append(high[0])
    return before, after


def segments(firsts, offsets):
    out, at = [], 0
    for first in firsts:
        out.append((at, offsets - first))
        at += offsets - first
    return out, at


def spec():
    return pl.BlockSpec(memory_space=pltpu.VMEM)


def cost(flops, moved):
    return pl.CostEstimate(flops=flops, bytes_accessed=moved, transcendentals=0)


def swap_matrix(offsets, columns):
    n = offsets * columns
    row = lax.broadcasted_iota(jnp.int32, (n, n), 0)
    col = lax.broadcasted_iota(jnp.int32, (n, n), 1)
    hit = col == (row % offsets) * columns + row // offsets
    return jnp.where(hit, 1.0, 0.0).astype(BF)


def to_columns(swap, planes):
    h, x, y = planes.shape
    moved = jnp.dot(swap, planes.reshape(h * x, y), preferred_element_type=F32)
    return moved.astype(BF).reshape(x, h, y)


def pack_kernel(before, after, image, up, down):
    h, z = image.shape[:2]
    for k, (at, n) in enumerate(segments(before, h)[0]):
        up[at : at + n] = image[h - n : h, z - 1 - k]
    for k, (at, n) in enumerate(segments(after, h)[0]):
        down[at : at + n] = image[h - n : h, k]


def pack(image, before, after):
    h, z, x, y = image.shape
    n_up, n_down = segments(before, h)[1], segments(after, h)[1]
    return pl.pallas_call(
        functools.partial(pack_kernel, before, after),
        out_shape=(
            jax.ShapeDtypeStruct((n_up, x, y), BF),
            jax.ShapeDtypeStruct((n_down, x, y), BF),
        ),
        in_specs=[spec()],
        out_specs=(spec(), spec()),
        name="pack",
    )(image)


def local_kernel(image, coefficients, dip, columns, weights):
    h, z, x, y = image.shape
    swap = swap_matrix(h, x)
    for level in range(z):
        columns[:, level * h : (level + 1) * h, :] = to_columns(swap, image[:, level])
    lane = lax.broadcasted_iota(jnp.int32, (z * x, y), 1)
    classes = dip[...]
    tests = [classes == q for q in range(1, coefficients.shape[0])]
    for t in range(weights.shape[0]):
        w = jnp.full((z * x, y), coefficients[0, t], F32)
        for q, test in enumerate(tests):
            w = jnp.where(test, coefficients[q + 1, t], w)
        shift = t % (2 * RY + 1) - RY
        if shift:
            w = pltpu.roll(w, shift % y, 1)
            w = jnp.where(lane < shift if shift > 0 else lane >= y + shift, 0.0, w)
        weights[t] = w


def prepare(image, coefficients, dip):
    h, z, x, y = image.shape
    taps = coefficients.shape[1]
    return pl.pallas_call(
        local_kernel,
        out_shape=(
            jax.ShapeDtypeStruct((x, z * h, y), BF),
            jax.ShapeDtypeStruct((taps, z * x, y), F32),
        ),
        in_specs=[spec(), pl.BlockSpec(memory_space=pltpu.SMEM), spec()],
        out_specs=(spec(), spec()),
        cost_estimate=cost(2 * h * x * h * x * y * z, 8 << 20),
        name="prepare",
    )(image, coefficients, dip.reshape(z * x, y))


def stack_block(slant, low, mid, high, zb, x, tile):
    n_low = low.shape[1] - zb * tile
    n_mid = mid.shape[1]
    n_high = (zb + 1) * tile
    total = jnp.dot(slant[:, :n_low], low[x, zb * tile :, :], preferred_element_type=F32)
    total += jnp.dot(slant[:, n_low : n_low + n_mid], mid[x], preferred_element_type=F32)
    total += jnp.dot(slant[:, n_low + n_mid :], high[x, :n_high, :], preferred_element_type=F32)
    return total.astype(BF)


def first_kernel(before, after, slant, up, down, mid, gathers, low, high):
    h = slant.shape[1] // (2 * R + ZB)
    x = mid.shape[0]
    swap = swap_matrix(h, x)
    for k, (at, n) in enumerate(segments(before, h)[0]):
        plane = to_columns(swap, up[at + n - h : at + n])
        low[:, (R - 1 - k) * h : (R - k) * h, :] = plane
    for k, (at, n) in enumerate(segments(after, h)[0]):
        high[:, k * h : (k + 1) * h, :] = to_columns(swap, down[at + n - h : at + n])
    for k in range(len(after), R):
        high[:, k * h : (k + 1) * h, :] = jnp.zeros((x, h, high.shape[2]), BF)
    for column in range(x):
        gathers[column] = stack_block(slant, low, mid, high, 0, column, ZB * h)


def first_gathers(slant, up, down, mid, before, after):
    x, rows, y = mid.shape
    m = slant.shape[0]
    return pl.pallas_call(
        functools.partial(first_kernel, before, after),
        out_shape=(
            jax.ShapeDtypeStruct((x, m, y), BF),
            jax.ShapeDtypeStruct((x, rows, y), BF),
            jax.ShapeDtypeStruct((x, rows, y), BF),
        ),
        in_specs=[spec()] * 4,
        out_specs=(spec(),) * 3,
        cost_estimate=cost(2 * m * slant.shape[1] * x * y, 10 << 20),
        name="first",
    )(slant, up, down, mid)


def rest_kernel(slant, low, mid, high, *outs):
    h = slant.shape[1] // (2 * R + ZB)
    for n, out in enumerate(outs):
        for column in range(mid.shape[0]):
            out[column] = stack_block(slant, low, mid, high, n + 1, column, ZB * h)


def rest_gathers(slant, low, mid, high, count):
    x, rows, y = mid.shape
    m = slant.shape[0]
    return pl.pallas_call(
        rest_kernel,
        out_shape=(jax.ShapeDtypeStruct((x, m, y), BF),) * count,
        in_specs=[spec()] * 4,
        out_specs=(spec(),) * count,
        cost_estimate=cost(2 * count * m * slant.shape[1] * x * y, 9 << 20),
        name="rest",
    )(slant, low, mid, high)


def smooth_kernel(angles, weights, previous, own, following, *rest):
    out, scratch = rest[-2:]
    x, _, y = own.shape
    sources = (previous, own, following)
    n = angles * x
    row = lax.broadcasted_iota(jnp.int32, (n, n), 0)
    col = lax.broadcasted_iota(jnp.int32, (n, n), 1)
    swap = jnp.where(row == (col % angles) * x + col // angles, 1.0, 0.0).astype(BF)
    part = 32

    def level(j, carry):
        for column in range(x):
            for piece in range(angles // part):
                sums = [jnp.zeros((part, y), F32) for _ in range(2 * RY + 1)]
                for step in range(2 * RX + 1):
                    source = column + step - RX + x
                    rows = pl.ds(pl.multiple_of(j * angles + piece * part, part), part)
                    values = sources[source // x][source % x, rows, :].astype(F32)
                    for side in range(2 * RY + 1):
                        w = weights[step * (2 * RY + 1) + side, pl.ds(j * x + column, 1), :]
                        sums[side] = sums[side] + w * values
                total = sums[RY]
                for side in range(2 * RY + 1):
                    if side != RY:
                        total = total + pltpu.roll(sums[side], (RY - side) % y, 1)
                at = column * angles + piece * part
                scratch[at : at + part, :] = total.astype(BF)
        moved = jnp.dot(swap, scratch[...], preferred_element_type=F32)
        out[:, j] = moved.astype(BF).reshape(angles, x, y)
        return carry

    lax.fori_loop(0, ZB, level, 0)


def smooth(weights, previous, own, following, done, block, shape):
    angles, z, x, y = shape
    taps = weights.shape[0]
    whole = pl.BlockSpec(own.shape, lambda i: (0, 0, 0))
    in_specs = [pl.BlockSpec((taps, ZB * x, y), lambda i: (0, block, 0)), whole, whole, whole]
    operands = [weights, previous, own, following]
    aliases = {}
    if done is not None:
        in_specs.append(pl.BlockSpec(memory_space=pl.ANY))
        operands.append(done)
        aliases = {4: 0}
    return pl.pallas_call(
        functools.partial(smooth_kernel, angles),
        grid=(1,),
        out_shape=jax.ShapeDtypeStruct(shape, BF),
        in_specs=in_specs,
        out_specs=pl.BlockSpec((angles, ZB, x, y), lambda i: (0, block, 0, 0)),
        scratch_shapes=[pltpu.VMEM((angles * x, y), BF)],
        input_output_aliases=aliases,
        cost_estimate=cost(2 * taps * angles * ZB * x * y, 3 << 20),
        name="smooth",
    )(*operands)


def slant_matrix_of(slant_taper, band_offsets, offset_count):
    offset_index = jnp.arange(offset_count, dtype=jnp.int32)
    depth_shift = jnp.floor_divide(band_offsets[:, None] * offset_index[None, :], offset_count)
    reach_index = jnp.arange(slant_taper.shape[2], dtype=jnp.int32) - R
    inside_band = jnp.abs(reach_index[None, None, :] - depth_shift[:, :, None]) <= BAND
    return jnp.where(inside_band, slant_taper, jnp.zeros_like(slant_taper))


def block_matrix(slant_taper, band_offsets, offset_count):
    slant = slant_matrix_of(slant_taper, band_offsets, offset_count)
    angles, h, steps = slant.shape
    flat = jnp.transpose(slant, (0, 2, 1)).reshape(angles, steps * h)
    rows = [jnp.pad(flat, ((0, 0), (j * h, (ZB - 1 - j) * h))) for j in range(ZB)]
    return jnp.concatenate(rows, axis=0)


def exchange(x_up, x_down, axis):
    count = lax.axis_size(axis)
    up = [(i, i + 1) for i in range(count - 1)]
    down = [(j, i) for i, j in up]
    return lax.ppermute(x_up, axis, up), lax.ppermute(x_down, axis, down)


def local(offset_image, dip_class, slant_taper, band_offsets, coefficients):
    h, z, x, y = offset_image.shape
    angles = slant_taper.shape[0]
    before, after = reach_tables(h, R)
    up, down = pack(offset_image, before, after)
    up, down = exchange(up, down, "depth")
    mid, weights = prepare(offset_image, coefficients, dip_class)
    slant = block_matrix(slant_taper, band_offsets, h)
    first, low, high = first_gathers(slant, up, down, mid, before, after)
    blocks = z // ZB
    others = rest_gathers(slant, low, mid, high, blocks - 1)
    done = None
    for block, own in enumerate((first, *others)):
        previous, following = exchange(own, own, "gx")
        done = smooth(weights, previous, own, following, done, block, (angles, z, x, y))
    return done


def solution(mesh):
    return jax.shard_map(
        local,
        mesh=mesh,
        in_specs=(P(None, "depth", "gx", None), P("depth", "gx", None), P(), P(), P()),
        out_specs=P(None, "depth", "gx", None),
        check_vma=False,
    )
```

```python
import functools

import jax
import jax.numpy as jnp
from jax import lax
from jax.experimental import pallas as pl
from jax.experimental.pallas import tpu as pltpu
from jax.sharding import PartitionSpec as P

R = 16
BAND = 2
RX = 4
RY = 1
REACH = R - BAND
ZB = 4
BF = jnp.bfloat16
F32 = jnp.float32


def reach_tables(offsets, steps):
    before, after = [], []
    for k in range(1, steps + 1):
        low = [h for h in range(offsets) if -((-REACH * h) // offsets) + BAND >= k]
        high = [h for h in range(offsets) if (REACH * h) // offsets + BAND >= k]
        if low:
            before.append(low[0])
        if high:
            after.append(high[0])
    return before, after


def segments(firsts, offsets):
    out, at = [], 0
    for first in firsts:
        out.append((at, offsets - first))
        at += offsets - first
    return out, at


def spec():
    return pl.BlockSpec(memory_space=pltpu.VMEM)


def cost(flops, moved):
    return pl.CostEstimate(flops=flops, bytes_accessed=moved, transcendentals=0)


def swap_matrix(offsets, columns):
    n = offsets * columns
    row = lax.broadcasted_iota(jnp.int32, (n, n), 0)
    col = lax.broadcasted_iota(jnp.int32, (n, n), 1)
    hit = col == (row % offsets) * columns + row // offsets
    return jnp.where(hit, 1.0, 0.0).astype(BF)


def to_columns(swap, planes):
    h, x, y = planes.shape
    moved = jnp.dot(swap, planes.reshape(h * x, y), preferred_element_type=F32)
    return moved.astype(BF).reshape(x, h, y)


def pack_kernel(before, after, image, up, down):
    h, z = image.shape[:2]
    for k, (at, n) in enumerate(segments(before, h)[0]):
        up[at : at + n] = image[h - n : h, z - 1 - k]
    for k, (at, n) in enumerate(segments(after, h)[0]):
        down[at : at + n] = image[h - n : h, k]


def pack(image, before, after):
    h, z, x, y = image.shape
    n_up, n_down = segments(before, h)[1], segments(after, h)[1]
    return pl.pallas_call(
        functools.partial(pack_kernel, before, after),
        out_shape=(
            jax.ShapeDtypeStruct((n_up, x, y), BF),
            jax.ShapeDtypeStruct((n_down, x, y), BF),
        ),
        in_specs=[spec()],
        out_specs=(spec(), spec()),
        compiler_params=pltpu.CompilerParams(vmem_limit_bytes=16 << 20),
        name="pack",
    )(image)


def local_kernel(image, coefficients, dip, columns, weights):
    h, z, x, y = image.shape
    swap = swap_matrix(h, x)
    for level in range(z):
        columns[:, level * h : (level + 1) * h, :] = to_columns(swap, image[:, level])
    lane = lax.broadcasted_iota(jnp.int32, (z * x, y), 1)
    classes = dip[...]
    tests = [classes == q for q in range(1, coefficients.shape[0])]
    for t in range(weights.shape[0]):
        w = jnp.full((z * x, y), coefficients[0, t], F32)
        for q, test in enumerate(tests):
            w = jnp.where(test, coefficients[q + 1, t], w)
        shift = t % (2 * RY + 1) - RY
        if shift:
            w = pltpu.roll(w, shift % y, 1)
            w = jnp.where(lane < shift if shift > 0 else lane >= y + shift, 0.0, w)
        weights[t] = w


def prepare(image, coefficients, dip):
    h, z, x, y = image.shape
    taps = coefficients.shape[1]
    return pl.pallas_call(
        local_kernel,
        out_shape=(
            jax.ShapeDtypeStruct((x, z * h, y), BF),
            jax.ShapeDtypeStruct((taps, z * x, y), F32),
        ),
        in_specs=[spec(), pl.BlockSpec(memory_space=pltpu.SMEM), spec()],
        out_specs=(spec(), spec()),
        cost_estimate=cost(2 * h * x * h * x * y * z, 8 << 20),
        compiler_params=pltpu.CompilerParams(vmem_limit_bytes=16 << 20),
        name="prepare",
    )(image, coefficients, dip.reshape(z * x, y))


def stack_block(slant, low, mid, high, zb, x, tile):
    n_low = low.shape[1] - zb * tile
    n_mid = mid.shape[1]
    n_high = (zb + 1) * tile
    total = jnp.dot(slant[:, :n_low], low[x, zb * tile :, :], preferred_element_type=F32)
    total += jnp.dot(slant[:, n_low : n_low + n_mid], mid[x], preferred_element_type=F32)
    total += jnp.dot(slant[:, n_low + n_mid :], high[x, :n_high, :], preferred_element_type=F32)
    return total.astype(BF)


def first_kernel(before, after, slant, up, down, mid, gathers, low, high):
    h = slant.shape[1] // (2 * R + ZB)
    x = mid.shape[0]
    swap = swap_matrix(h, x)
    for k, (at, n) in enumerate(segments(before, h)[0]):
        plane = to_columns(swap, up[at + n - h : at + n])
        low[:, (R - 1 - k) * h : (R - k) * h, :] = plane
    for k, (at, n) in enumerate(segments(after, h)[0]):
        high[:, k * h : (k + 1) * h, :] = to_columns(swap, down[at + n - h : at + n])
    for k in range(len(after), R):
        high[:, k * h : (k + 1) * h, :] = jnp.zeros((x, h, high.shape[2]), BF)
    for column in range(x):
        gathers[column] = stack_block(slant, low, mid, high, 0, column, ZB * h)


def first_gathers(slant, up, down, mid, before, after):
    x, rows, y = mid.shape
    m = slant.shape[0]
    return pl.pallas_call(
        functools.partial(first_kernel, before, after),
        out_shape=(
            jax.ShapeDtypeStruct((x, m, y), BF),
            jax.ShapeDtypeStruct((x, rows, y), BF),
            jax.ShapeDtypeStruct((x, rows, y), BF),
        ),
        in_specs=[spec()] * 4,
        out_specs=(spec(),) * 3,
        cost_estimate=cost(2 * m * slant.shape[1] * x * y, 10 << 20),
        compiler_params=pltpu.CompilerParams(vmem_limit_bytes=20 << 20),
        name="first",
    )(slant, up, down, mid)


def rest_kernel(slant, low, mid, high, *outs):
    h = slant.shape[1] // (2 * R + ZB)
    for n, out in enumerate(outs):
        for column in range(mid.shape[0]):
            out[column] = stack_block(slant, low, mid, high, n + 1, column, ZB * h)


def rest_gathers(slant, low, mid, high, count):
    x, rows, y = mid.shape
    m = slant.shape[0]
    return pl.pallas_call(
        rest_kernel,
        out_shape=(jax.ShapeDtypeStruct((x, m, y), BF),) * count,
        in_specs=[spec()] * 4,
        out_specs=(spec(),) * count,
        cost_estimate=cost(2 * count * m * slant.shape[1] * x * y, 9 << 20),
        compiler_params=pltpu.CompilerParams(vmem_limit_bytes=20 << 20),
        name="rest",
    )(slant, low, mid, high)


def smooth_kernel(angles, weights, previous, own, following, *rest):
    out, scratch = rest[-2:]
    x, _, y = own.shape
    sources = (previous, own, following)
    n = angles * x
    row = lax.broadcasted_iota(jnp.int32, (n, n), 0)
    col = lax.broadcasted_iota(jnp.int32, (n, n), 1)
    swap = jnp.where(row == (col % angles) * x + col // angles, 1.0, 0.0).astype(BF)
    part = 32

    def level(j, carry):
        for column in range(x):
            for piece in range(angles // part):
                sums = [jnp.zeros((part, y), F32) for _ in range(2 * RY + 1)]
                for step in range(2 * RX + 1):
                    source = column + step - RX + x
                    rows = pl.ds(pl.multiple_of(j * angles + piece * part, part), part)
                    values = sources[source // x][source % x, rows, :].astype(F32)
                    for side in range(2 * RY + 1):
                        w = weights[step * (2 * RY + 1) + side, pl.ds(j * x + column, 1), :]
                        sums[side] = sums[side] + w * values
                total = sums[RY]
                for side in range(2 * RY + 1):
                    if side != RY:
                        total = total + pltpu.roll(sums[side], (RY - side) % y, 1)
                at = column * angles + piece * part
                scratch[at : at + part, :] = total.astype(BF)
        moved = jnp.dot(swap, scratch[...], preferred_element_type=F32)
        out[:, j] = moved.astype(BF).reshape(angles, x, y)
        return carry

    lax.fori_loop(0, ZB, level, 0)


def smooth(weights, previous, own, following, done, block, shape):
    angles, z, x, y = shape
    taps = weights.shape[0]
    whole = pl.BlockSpec(own.shape, lambda i: (0, 0, 0))
    in_specs = [pl.BlockSpec((taps, ZB * x, y), lambda i: (0, block, 0)), whole, whole, whole]
    operands = [weights, previous, own, following]
    aliases = {}
    if done is not None:
        in_specs.append(pl.BlockSpec(memory_space=pl.ANY))
        operands.append(done)
        aliases = {4: 0}
    return pl.pallas_call(
        functools.partial(smooth_kernel, angles),
        grid=(1,),
        out_shape=jax.ShapeDtypeStruct(shape, BF),
        in_specs=in_specs,
        out_specs=pl.BlockSpec((angles, ZB, x, y), lambda i: (0, block, 0, 0)),
        scratch_shapes=[pltpu.VMEM((angles * x, y), BF)],
        input_output_aliases=aliases,
        cost_estimate=cost(2 * taps * angles * ZB * x * y, 3 << 20),
        compiler_params=pltpu.CompilerParams(vmem_limit_bytes=16 << 20),
        name="smooth",
    )(*operands)


def slant_matrix_of(slant_taper, band_offsets, offset_count):
    offset_index = jnp.arange(offset_count, dtype=jnp.int32)
    depth_shift = jnp.floor_divide(band_offsets[:, None] * offset_index[None, :], offset_count)
    reach_index = jnp.arange(slant_taper.shape[2], dtype=jnp.int32) - R
    inside_band = jnp.abs(reach_index[None, None, :] - depth_shift[:, :, None]) <= BAND
    return jnp.where(inside_band, slant_taper, jnp.zeros_like(slant_taper))


def block_matrix(slant_taper, band_offsets, offset_count):
    slant = slant_matrix_of(slant_taper, band_offsets, offset_count)
    angles, h, steps = slant.shape
    flat = jnp.transpose(slant, (0, 2, 1)).reshape(angles, steps * h)
    rows = [jnp.pad(flat, ((0, 0), (j * h, (ZB - 1 - j) * h))) for j in range(ZB)]
    return jnp.concatenate(rows, axis=0)


def exchange(x_up, x_down, axis):
    count = lax.axis_size(axis)
    up = [(i, i + 1) for i in range(count - 1)]
    down = [(j, i) for i, j in up]
    return lax.ppermute(x_up, axis, up), lax.ppermute(x_down, axis, down)


def local(offset_image, dip_class, slant_taper, band_offsets, coefficients):
    h, z, x, y = offset_image.shape
    angles = slant_taper.shape[0]
    before, after = reach_tables(h, R)
    up, down = pack(offset_image, before, after)
    up, down = exchange(up, down, "depth")
    mid, weights = prepare(offset_image, coefficients, dip_class)
    slant = block_matrix(slant_taper, band_offsets, h)
    first, low, high = first_gathers(slant, up, down, mid, before, after)
    blocks = z // ZB
    others = rest_gathers(slant, low, mid, high, blocks - 1)
    done = None
    for block, own in enumerate((first, *others)):
        previous, following = exchange(own, own, "gx")
        done = smooth(weights, previous, own, following, done, block, (angles, z, x, y))
    return done


def solution(mesh):
    return jax.shard_map(
        local,
        mesh=mesh,
        in_specs=(P(None, "depth", "gx", None), P("depth", "gx", None), P(), P(), P()),
        out_specs=P(None, "depth", "gx", None),
        check_vma=False,
    )
```

```python
import functools

import jax
import jax.numpy as jnp
from jax import lax
from jax.experimental import pallas as pl
from jax.experimental.pallas import tpu as pltpu
from jax.sharding import PartitionSpec as P

R = 16
BAND = 2
RX = 4
RY = 1
REACH = R - BAND
ZB = 4
HALVES = 2
LAST_PARTS = (8, 8)
PART = 32
SIDES = 2 * RY + 1
BF = jnp.bfloat16
F32 = jnp.float32


def reach_tables(offsets, steps):
    before, after = [], []
    for k in range(1, steps + 1):
        low = [h for h in range(offsets) if -((-REACH * h) // offsets) + BAND >= k]
        high = [h for h in range(offsets) if (REACH * h) // offsets + BAND >= k]
        if low:
            before.append(low[0])
        if high:
            after.append(high[0])
    return before, after


def segments(firsts, offsets):
    out, at = [], 0
    for first in firsts:
        out.append((at, offsets - first))
        at += offsets - first
    return out, at


def spec():
    return pl.BlockSpec(memory_space=pltpu.VMEM)


def params(mib):
    return pltpu.CompilerParams(vmem_limit_bytes=mib << 20)


def cost(flops, moved):
    return pl.CostEstimate(flops=flops, bytes_accessed=moved, transcendentals=0)


def struct(shape, kind=BF):
    return jax.ShapeDtypeStruct(shape, kind)


def swap_matrix(offsets, columns):
    n = offsets * columns
    row = lax.broadcasted_iota(jnp.int32, (n, n), 0)
    col = lax.broadcasted_iota(jnp.int32, (n, n), 1)
    hit = col == (row % offsets) * columns + row // offsets
    return jnp.where(hit, 1.0, 0.0).astype(BF)


def unswap_matrix(angles, columns):
    n = angles * columns
    row = lax.broadcasted_iota(jnp.int32, (n, n), 0)
    col = lax.broadcasted_iota(jnp.int32, (n, n), 1)
    hit = row == (col % angles) * columns + col // angles
    return jnp.where(hit, 1.0, 0.0).astype(BF)


def pack_half(before, after, half, image, up, down):
    h, z, _, y = image.shape
    width = y // HALVES
    lanes = slice(half * width, (half + 1) * width)
    for k, (at, n) in enumerate(segments(before, h)[0]):
        up[at : at + n] = image[h - n : h, z - 1 - k, :, lanes]
    for k, (at, n) in enumerate(segments(after, h)[0]):
        down[at : at + n] = image[h - n : h, k, :, lanes]


def pack_shapes(image, before, after):
    h, _, x, y = image.shape
    n_up, n_down = segments(before, h)[1], segments(after, h)[1]
    return struct((n_up, x, y // HALVES)), struct((n_down, x, y // HALVES))


def pack(image, before, after):
    return pl.pallas_call(
        functools.partial(pack_half, before, after, 0),
        out_shape=pack_shapes(image, before, after),
        in_specs=[spec()],
        out_specs=(spec(),) * 2,
        compiler_params=params(16),
        name="pack",
    )(image)


def prepare_kernel(before, after, image, coefficients, dip, slant, up, down, *outs):
    columns, (matrix, weights) = outs[:HALVES], outs[HALVES:]
    h, z, x, y = image.shape
    width = y // HALVES
    pack_half(before, after, 1, image, up, down)
    swap = swap_matrix(h, x)
    for level in range(z):
        plane = image[:, level].reshape(h * x, y)
        moved = jnp.dot(swap, plane, preferred_element_type=F32).astype(BF)
        for half in range(HALVES):
            for c in range(x):
                at = (c % 2) * width
                columns[half][c // 2, level * h : (level + 1) * h, at : at + width] = moved[
                    c * h : (c + 1) * h, half * width : (half + 1) * width
                ]
    steps, angles, _ = slant.shape
    zero = jnp.zeros((angles, h), BF)
    for j in range(ZB):
        for t in range((steps + ZB - 1) // 2):
            pair = [slant[d] if 0 <= d < steps else zero for d in (2 * t - j, 2 * t + 1 - j)]
            matrix[j * angles : (j + 1) * angles, 2 * t * h : 2 * (t + 1) * h] = jnp.concatenate(
                pair, axis=1
            )
    lane = lax.broadcasted_iota(jnp.int32, (z * x, y), 1)
    classes = dip[...]
    tests = [classes == q for q in range(1, coefficients.shape[0])]
    for t in range(weights.shape[1]):
        w = jnp.full((z * x, y), coefficients[0, t], F32)
        for q, test in enumerate(tests):
            w = jnp.where(test, coefficients[q + 1, t], w)
        shift = t % SIDES - RY
        if shift:
            w = pltpu.roll(w, shift % y, 1)
            w = jnp.where(lane < shift if shift > 0 else lane >= y + shift, 0.0, w)
        for half in range(HALVES):
            weights[half, t] = w[:, half * width : (half + 1) * width]


def prepare(image, coefficients, dip, slant, before, after):
    h, z, x, y = image.shape
    steps, angles, _ = slant.shape
    taps = coefficients.shape[1]
    return pl.pallas_call(
        functools.partial(prepare_kernel, before, after),
        out_shape=(
            *pack_shapes(image, before, after),
            *(struct((x // 2, z * h, 2 * y // HALVES)) for _ in range(HALVES)),
            struct((ZB * angles, (steps + ZB - 1) * h)),
            struct((HALVES, taps, z * x, y // HALVES), F32),
        ),
        in_specs=[spec(), pl.BlockSpec(memory_space=pltpu.SMEM), spec(), spec()],
        out_specs=(spec(),) * (4 + HALVES),
        compiler_params=params(24),
        cost_estimate=cost(2 * h * x * h * x * y * z, 8 << 20),
        name="prepare",
    )(image, coefficients, dip.reshape(z * x, y), slant)


def unpack(swap, source, pieces, starts, target):
    h, x = swap.shape[0] // source.shape[1], source.shape[1]
    width = source.shape[2]
    for k in range(0, len(pieces), 2):
        pair = [pieces[min(i, len(pieces) - 1)] for i in (k, k + 1)]
        planes = [source[at + n - h : at + n].reshape(h * x, width) for at, n in pair]
        moved = jnp.dot(swap, jnp.concatenate(planes, axis=1), preferred_element_type=F32)
        moved = moved.astype(BF)
        for i in range(min(2, len(pieces) - k)):
            rows = slice(starts[k + i] * h, (starts[k + i] + 1) * h)
            for c in range(x):
                at = (c % 2) * width
                target[c // 2, rows, at : at + width] = moved[
                    c * h : (c + 1) * h, i * width : (i + 1) * width
                ]


def gather_kernel(before, after, parts, matrix, up, down, mid, *rest):
    outs, (low, high) = rest[: len(parts)], rest[len(parts) :]
    x = up.shape[1]
    m = matrix.shape[0]
    h = matrix.shape[1] // (2 * R + ZB)
    tile = ZB * h
    swap = swap_matrix(h, x)
    unpack(swap, up, segments(before, h)[0], [R - 1 - k for k in range(R)], low)
    unpack(swap, down, segments(after, h)[0], list(range(R)), high)
    for k in range(len(after), R):
        high[:, k * h : (k + 1) * h, :] = jnp.zeros((x // 2, h, high.shape[2]), BF)
    zb = 0
    n_mid = mid.shape[1]
    for out, planes in zip(outs, parts):
        for block in range(planes // ZB):
            n_low = low.shape[1] - zb * tile
            n_high = (zb + 1) * tile
            for c in range(x // 2):
                total = jnp.dot(
                    matrix[:, n_low : n_low + n_mid], mid[c], preferred_element_type=F32
                )
                total += jnp.dot(
                    matrix[:, :n_low], low[c, zb * tile :, :], preferred_element_type=F32
                )
                total += jnp.dot(
                    matrix[:, n_low + n_mid :], high[c, :n_high, :], preferred_element_type=F32
                )
                out[c, block * m : (block + 1) * m, :] = total.astype(BF)
            zb += 1


def gather(matrix, up, down, mid, before, after, parts):
    pairs, rows, width = mid.shape
    per_plane = matrix.shape[0] // ZB
    return pl.pallas_call(
        functools.partial(gather_kernel, before, after, parts),
        out_shape=tuple(struct((pairs, n * per_plane, width)) for n in parts),
        in_specs=[spec()] * 4,
        out_specs=(spec(),) * len(parts),
        scratch_shapes=[pltpu.VMEM((pairs, rows, width), BF)] * 2,
        compiler_params=params(24),
        cost_estimate=cost(2 * sum(parts) * per_plane * matrix.shape[1] * pairs * width, 6 << 20),
        name="gather",
    )(matrix, up, down, mid)


def half_sums(weights, sources, row, at, column, x, half):
    width = sources[0].shape[2] // 2
    sums = [None] * SIDES
    for step in range(2 * RX + 1):
        n = column + step - RX + x
        source, c = sources[n // x], n % x
        side_at = (c % 2) * width
        values = source[c // 2, pl.ds(at, PART), side_at : side_at + width].astype(F32)
        for side in range(SIDES):
            w = weights[half, step * SIDES + side, pl.ds(row, 1), :]
            term = w * values
            sums[side] = term if sums[side] is None else sums[side] + term
    return sums


def spread(sums, half):
    zero = jnp.zeros_like(sums[0])
    total = None
    for side in range(SIDES):
        both = jnp.concatenate([sums[side], zero] if half == 0 else [zero, sums[side]], axis=1)
        if side != RY:
            both = pltpu.roll(both, (RY - side) % both.shape[1], 1)
        total = both if total is None else total + both
    return total


def smooth_a_kernel(angles, x, weights, previous, own, following, totals):
    sources = (previous, own, following)

    def level(j, carry):
        for column in range(x):
            for piece in range(angles // PART):
                at = pl.multiple_of(j * angles + piece * PART, PART)
                row = j * x + column
                sums = half_sums(weights, sources, row, at, column, x, 0)
                totals[row, piece * PART : (piece + 1) * PART, :] = spread(sums, 0)
        return carry

    lax.fori_loop(0, totals.shape[0] // x, level, 0)


def smooth_a(weights, previous, own, following, angles, z, x, y):
    return pl.pallas_call(
        functools.partial(smooth_a_kernel, angles, x),
        out_shape=struct((z * x, angles, y), F32),
        in_specs=[spec()] * 4,
        out_specs=spec(),
        compiler_params=params(20),
        cost_estimate=cost(weights.shape[1] * angles * z * x * y, 10 << 20),
        name="smooth_a",
    )(weights, previous, own, following)


def smooth_b_kernel(angles, x, first, weights, totals, previous, own, following, *rest):
    out, scratch = rest[-2:]
    sources = (previous, own, following)
    unswap = unswap_matrix(angles, x)
    y = out.shape[3]
    base = pl.program_id(0) * ZB

    def level(j, carry):
        for column in range(x):
            for piece in range(angles // PART):
                at = pl.multiple_of((base + j) * angles + piece * PART, PART)
                row = (first + base + j) * x + column
                sums = half_sums(weights, sources, row, at, column, x, 1)
                part = slice(piece * PART, (piece + 1) * PART)
                total = totals[row, part, :] + spread(sums, 1)
                to = column * angles + piece * PART
                scratch[to : to + PART, :] = total.astype(BF)
        moved = jnp.dot(unswap, scratch[...], preferred_element_type=F32)
        out[:, j] = moved.astype(BF).reshape(angles, x, y)
        return carry

    lax.fori_loop(0, ZB, level, 0)


def smooth_b(weights, totals, previous, own, following, done, first, shape):
    angles, z, x, y = shape
    planes = own.shape[1] // angles
    in_specs = [spec()] * 5
    operands = [weights, totals, previous, own, following]
    aliases = {}
    if done is not None:
        in_specs.append(pl.BlockSpec(memory_space=pl.ANY))
        operands.append(done)
        aliases = {5: 0}
    return pl.pallas_call(
        functools.partial(smooth_b_kernel, angles, x, first),
        grid=(planes // ZB,),
        out_shape=struct(shape),
        in_specs=in_specs,
        out_specs=pl.BlockSpec((angles, ZB, x, y), lambda i: (0, first // ZB + i, 0, 0)),
        scratch_shapes=[pltpu.VMEM((angles * x, y), BF)],
        input_output_aliases=aliases,
        compiler_params=params(20),
        cost_estimate=cost(weights.shape[1] * angles * planes * x * y, 3 << 20),
        name="smooth_b",
    )(*operands)


def slant_matrix_of(slant_taper, band_offsets, offset_count):
    offset_index = jnp.arange(offset_count, dtype=jnp.int32)
    depth_shift = jnp.floor_divide(band_offsets[:, None] * offset_index[None, :], offset_count)
    reach_index = jnp.arange(slant_taper.shape[2], dtype=jnp.int32) - R
    inside_band = jnp.abs(reach_index[None, None, :] - depth_shift[:, :, None]) <= BAND
    return jnp.where(inside_band, slant_taper, jnp.zeros_like(slant_taper))


def exchange(x_up, x_down, axis):
    count = lax.axis_size(axis)
    up = [(i, i + 1) for i in range(count - 1)]
    down = [(j, i) for i, j in up]
    return lax.ppermute(x_up, axis, up), lax.ppermute(x_down, axis, down)


def local(offset_image, dip_class, slant_taper, band_offsets, coefficients):
    h, z, x, y = offset_image.shape
    angles = slant_taper.shape[0]
    before, after = reach_tables(h, R)
    up_a, down_a = exchange(*pack(offset_image, before, after), "depth")
    slant = jnp.transpose(slant_matrix_of(slant_taper, band_offsets, h), (2, 0, 1))
    prepared = prepare(offset_image, coefficients, dip_class, slant, before, after)
    up_b, down_b, mid_a, mid_b, matrix, weights = prepared
    up_b, down_b = exchange(up_b, down_b, "depth")
    (own_a,) = gather(matrix, up_a, down_a, mid_a, before, after, (z,))
    previous, following = exchange(own_a, own_a, "gx")
    owns = gather(matrix, up_b, down_b, mid_b, before, after, LAST_PARTS)
    totals = smooth_a(weights, previous, own_a, following, angles, z, x, y)
    done, first = None, 0
    for own, planes in zip(owns, LAST_PARTS):
        previous, following = exchange(own, own, "gx")
        done = smooth_b(
            weights, totals, previous, own, following, done, first, (angles, z, x, y)
        )
        first += planes
    return done


def solution(mesh):
    return jax.shard_map(
        local,
        mesh=mesh,
        in_specs=(P(None, "depth", "gx", None), P("depth", "gx", None), P(), P(), P()),
        out_specs=P(None, "depth", "gx", None),
        check_vma=False,
    )
```

```python
import functools

import jax
import jax.numpy as jnp
from jax import lax
from jax.experimental import pallas as pl
from jax.experimental.pallas import tpu as pltpu
from jax.sharding import PartitionSpec as P


R = 16
BAND = 2
RX = 4
RY = 1
REACH = R - BAND
ZB = 4
HALVES = 2
LAST_PARTS = (8, 8)
PART = 32
SIDES = 2 * RY + 1
BF = jnp.bfloat16
F32 = jnp.float32


def reach_tables(offsets, steps):
    before, after = [], []
    for k in range(1, steps + 1):
        low = [h for h in range(offsets) if -((-REACH * h) // offsets) + BAND >= k]
        high = [h for h in range(offsets) if (REACH * h) // offsets + BAND >= k]
        if low:
            before.append(low[0])
        if high:
            after.append(high[0])
    return before, after


def segments(firsts, offsets):
    out, at = [], 0
    for first in firsts:
        out.append((at, offsets - first))
        at += offsets - first
    return out, at


def spec():
    return pl.BlockSpec(memory_space=pltpu.VMEM)


def params(mib):
    return pltpu.CompilerParams(vmem_limit_bytes=mib << 20)


def cost(flops, moved):
    return pl.CostEstimate(flops=flops, bytes_accessed=moved, transcendentals=0)


def struct(shape, kind=BF):
    return jax.ShapeDtypeStruct(shape, kind)


def swap_matrix(offsets, columns):
    n = offsets * columns
    row = lax.broadcasted_iota(jnp.int32, (n, n), 0)
    col = lax.broadcasted_iota(jnp.int32, (n, n), 1)
    hit = col == (row % offsets) * columns + row // offsets
    return jnp.where(hit, 1.0, 0.0).astype(BF)


def unswap_matrix(angles, columns):
    n = angles * columns
    row = lax.broadcasted_iota(jnp.int32, (n, n), 0)
    col = lax.broadcasted_iota(jnp.int32, (n, n), 1)
    hit = row == (col % angles) * columns + col // angles
    return jnp.where(hit, 1.0, 0.0).astype(BF)


def pack_half(before, after, half, image, up, down):
    h, z, _, y = image.shape
    width = y // HALVES
    lanes = slice(half * width, (half + 1) * width)
    for k, (at, n) in enumerate(segments(before, h)[0]):
        up[at : at + n] = image[h - n : h, z - 1 - k, :, lanes]
    for k, (at, n) in enumerate(segments(after, h)[0]):
        down[at : at + n] = image[h - n : h, k, :, lanes]


def pack_shapes(image, before, after):
    h, _, x, y = image.shape
    n_up, n_down = segments(before, h)[1], segments(after, h)[1]
    return struct((n_up, x, y // HALVES)), struct((n_down, x, y // HALVES))


def pack(image, before, after):
    return pl.pallas_call(
        functools.partial(pack_half, before, after, 0),
        out_shape=pack_shapes(image, before, after),
        in_specs=[spec()],
        out_specs=(spec(),) * 2,
        compiler_params=params(14),
        name="pack",
    )(image)


def prepare_kernel(before, after, image, coefficients, dip, slant, up, down, *outs):
    columns, (matrix, weights) = outs[:HALVES], outs[HALVES:]
    h, z, x, y = image.shape
    width = y // HALVES
    pack_half(before, after, 1, image, up, down)
    swap = swap_matrix(h, x)
    for level in range(z):
        plane = image[:, level].reshape(h * x, y)
        moved = jnp.dot(swap, plane, preferred_element_type=F32).astype(BF)
        for half in range(HALVES):
            for c in range(x):
                at = (c % 2) * width
                columns[half][c // 2, level * h : (level + 1) * h, at : at + width] = moved[
                    c * h : (c + 1) * h, half * width : (half + 1) * width
                ]
    steps, angles, _ = slant.shape
    zero = jnp.zeros((angles, h), BF)
    for j in range(ZB):
        for t in range((steps + ZB - 1) // 2):
            pair = [slant[d] if 0 <= d < steps else zero for d in (2 * t - j, 2 * t + 1 - j)]
            matrix[j * angles : (j + 1) * angles, 2 * t * h : 2 * (t + 1) * h] = jnp.concatenate(
                pair, axis=1
            )
    lane = lax.broadcasted_iota(jnp.int32, (z * x, y), 1)
    classes = dip[...]
    tests = [classes == q for q in range(1, coefficients.shape[0])]
    for t in range(weights.shape[1]):
        w = jnp.full((z * x, y), coefficients[0, t], F32)
        for q, test in enumerate(tests):
            w = jnp.where(test, coefficients[q + 1, t], w)
        shift = t % SIDES - RY
        if shift:
            w = pltpu.roll(w, shift % y, 1)
            w = jnp.where(lane < shift if shift > 0 else lane >= y + shift, 0.0, w)
        for half in range(HALVES):
            weights[half, t] = w[:, half * width : (half + 1) * width]


def prepare(image, coefficients, dip, slant, before, after):
    h, z, x, y = image.shape
    steps, angles, _ = slant.shape
    taps = coefficients.shape[1]
    return pl.pallas_call(
        functools.partial(prepare_kernel, before, after),
        out_shape=(
            *pack_shapes(image, before, after),
            *(struct((x // 2, z * h, 2 * y // HALVES)) for _ in range(HALVES)),
            struct((ZB * angles, (steps + ZB - 1) * h)),
            struct((HALVES, taps, z * x, y // HALVES), F32),
        ),
        in_specs=[spec(), pl.BlockSpec(memory_space=pltpu.SMEM), spec(), spec()],
        out_specs=(spec(),) * (4 + HALVES),
        compiler_params=params(14),
        cost_estimate=cost(2 * h * x * h * x * y * z, 8 << 20),
        name="prepare",
    )(image, coefficients, dip.reshape(z * x, y), slant)


def unpack(swap, source, pieces, starts, target):
    h, x = swap.shape[0] // source.shape[1], source.shape[1]
    width = source.shape[2]
    for k in range(0, len(pieces), 2):
        pair = [pieces[min(i, len(pieces) - 1)] for i in (k, k + 1)]
        planes = [source[at + n - h : at + n].reshape(h * x, width) for at, n in pair]
        moved = jnp.dot(swap, jnp.concatenate(planes, axis=1), preferred_element_type=F32)
        moved = moved.astype(BF)
        for i in range(min(2, len(pieces) - k)):
            rows = slice(starts[k + i] * h, (starts[k + i] + 1) * h)
            for c in range(x):
                at = (c % 2) * width
                target[c // 2, rows, at : at + width] = moved[
                    c * h : (c + 1) * h, i * width : (i + 1) * width
                ]


def gather_kernel(before, after, parts, matrix, up, down, mid, *rest):
    (own, *outs), (low, high) = rest[:-2], rest[-2:]
    x = up.shape[1]
    m = matrix.shape[0]
    h = matrix.shape[1] // (2 * R + ZB)
    tile = ZB * h
    swap = swap_matrix(h, x)
    unpack(swap, up, segments(before, h)[0], [R - 1 - k for k in range(R)], low)
    unpack(swap, down, segments(after, h)[0], list(range(R)), high)
    for k in range(len(after), R):
        high[:, k * h : (k + 1) * h, :] = jnp.zeros((x // 2, h, high.shape[2]), BF)
    zb = 0
    n_mid = mid.shape[1]
    for index, planes in enumerate(parts):
        for block in range(planes // ZB):
            n_low = low.shape[1] - zb * tile
            n_high = (zb + 1) * tile
            for c in range(x // 2):
                total = jnp.dot(
                    matrix[:, n_low : n_low + n_mid], mid[c], preferred_element_type=F32
                )
                total += jnp.dot(
                    matrix[:, :n_low], low[c, zb * tile :, :], preferred_element_type=F32
                )
                total += jnp.dot(
                    matrix[:, n_low + n_mid :], high[c, :n_high, :], preferred_element_type=F32
                )
                moved = total.astype(BF)
                width = moved.shape[1] // 2
                for side in range(2):
                    piece = moved[:, side * width : (side + 1) * width]
                    own[2 * c + side, zb * m : (zb + 1) * m, :] = piece
                    if outs:
                        outs[index][2 * c + side, block * m : (block + 1) * m, :] = piece
            zb += 1


def gather(matrix, up, down, mid, before, after, parts):
    pairs, rows, width = mid.shape
    per_plane = matrix.shape[0] // ZB
    sizes = (sum(parts), *(parts if len(parts) > 1 else ()))
    return pl.pallas_call(
        functools.partial(gather_kernel, before, after, parts),
        out_shape=tuple(struct((2 * pairs, n * per_plane, width // 2)) for n in sizes),
        in_specs=[spec()] * 4,
        out_specs=(spec(),) * len(sizes),
        scratch_shapes=[pltpu.VMEM((pairs, rows, width), BF)] * 2,
        compiler_params=params(14),
        cost_estimate=cost(2 * sum(parts) * per_plane * matrix.shape[1] * pairs * width, 6 << 20),
        name="gather",
    )(matrix, up, down, mid)


def mirrored(n, count, flip):
    return n + flip * (count - 1 - 2 * n)


def half_sums(weights, half, row, at, terms):
    sums = [None] * SIDES
    for source, c, step in terms:
        values = source[c, pl.ds(at, PART), :].astype(F32)
        for side in range(SIDES):
            w = weights[half, step * SIDES + side, pl.ds(row, 1), :]
            term = w * values
            sums[side] = term if sums[side] is None else sums[side] + term
    return sums


def spread(sums, half):
    zero = jnp.zeros_like(sums[0])
    total = None
    for side in range(SIDES):
        both = jnp.concatenate([sums[side], zero] if half == 0 else [zero, sums[side]], axis=1)
        if side != RY:
            both = pltpu.roll(both, (RY - side) % both.shape[1], 1)
        total = both if total is None else total + both
    return total


def beside_terms(source, n, column, x, flip):
    terms = []
    for m in range(n + 1):
        c = mirrored(m, x, flip)
        terms.append((source, c, c - column + 2 * RX * (1 - flip)))
    return terms


def early_kernel(half, angles, x, flip_ref, weights, own, near, *rest):
    totals = rest[-1]
    flip = flip_ref[0]

    def level(j, carry):
        for n in range(x):
            column = mirrored(n, x, flip)
            row = j * x + column
            terms = [(own, c, c - column + RX) for c in range(x)]
            terms += beside_terms(near, n, column, x, flip)
            for piece in range(angles // PART):
                at = pl.multiple_of(j * angles + piece * PART, PART)
                part = slice(piece * PART, (piece + 1) * PART)
                total = spread(half_sums(weights, half, row, at, terms), half)
                if len(rest) > 1:
                    total = total + rest[0][row, part, :]
                totals[row, part, :] = total
        return carry

    lax.fori_loop(0, totals.shape[0] // x, level, 0)


def scalar_spec():
    return pl.BlockSpec(memory_space=pltpu.SMEM)


def early(flip, weights, own, near, totals, half, angles, z, x, y):
    operands = [flip, weights, own, near] + ([] if totals is None else [totals])
    return pl.pallas_call(
        functools.partial(early_kernel, half, angles, x),
        out_shape=struct((z * x, angles, y), F32),
        in_specs=[scalar_spec()] + [spec()] * (len(operands) - 1),
        out_specs=spec(),
        compiler_params=params(14),
        cost_estimate=cost(weights.shape[1] * angles * z * x * y, 10 << 20),
        name="early",
    )(*operands)


def add_far_kernel(angles, x, flip_ref, weights, far, given, totals):
    flip = flip_ref[0]

    def level(j, carry):
        for n in range(x):
            column = mirrored(n, x, flip)
            row = j * x + column
            terms = beside_terms(far, n, column, x, flip)
            for piece in range(angles // PART):
                at = pl.multiple_of(j * angles + piece * PART, PART)
                part = slice(piece * PART, (piece + 1) * PART)
                sums = half_sums(weights, 0, row, at, terms)
                totals[row, part, :] = given[row, part, :] + spread(sums, 0)
        return carry

    lax.fori_loop(0, totals.shape[0] // x, level, 0)


def add_far(flip, weights, far, totals, angles, z, x, y):
    return pl.pallas_call(
        functools.partial(add_far_kernel, angles, x),
        out_shape=struct((z * x, angles, y), F32),
        in_specs=[scalar_spec()] + [spec()] * 3,
        out_specs=spec(),
        compiler_params=params(14),
        cost_estimate=cost(weights.shape[1] * angles * z * x * y // 4, 8 << 20),
        name="add_far",
    )(flip, weights, far, totals)


def finish_kernel(angles, x, first, flip_ref, weights, totals, far, *rest):
    out, scratch = rest[-2:]
    flip = flip_ref[0]
    unswap = unswap_matrix(angles, x)
    base = pl.program_id(0) * ZB

    def level(j, carry):
        for n in range(x):
            column = mirrored(n, x, flip)
            row = (first + base + j) * x + column
            terms = beside_terms(far, n, column, x, flip)
            for piece in range(angles // PART):
                at = pl.multiple_of((base + j) * angles + piece * PART, PART)
                part = slice(piece * PART, (piece + 1) * PART)
                sums = half_sums(weights, 1, row, at, terms)
                total = totals[row, part, :] + spread(sums, 1)
                to = pl.multiple_of(column * angles + piece * PART, PART)
                scratch[pl.ds(to, PART), :] = total.astype(BF)
        moved = jnp.dot(unswap, scratch[...], preferred_element_type=F32)
        out[:, j] = moved.astype(BF).reshape(angles, x, out.shape[3])
        return carry

    lax.fori_loop(0, ZB, level, 0)


def finish(flip, weights, totals, far, done, first, shape):
    angles, _, x, y = shape
    planes = far.shape[1] // angles
    in_specs = [scalar_spec()] + [spec()] * 3
    operands = [flip, weights, totals, far]
    aliases = {}
    if done is not None:
        in_specs.append(pl.BlockSpec(memory_space=pl.ANY))
        operands.append(done)
        aliases = {4: 0}
    return pl.pallas_call(
        functools.partial(finish_kernel, angles, x, first),
        grid=(planes // ZB,),
        out_shape=struct(shape),
        in_specs=in_specs,
        out_specs=pl.BlockSpec((angles, ZB, x, y), lambda i: (0, first // ZB + i, 0, 0)),
        scratch_shapes=[pltpu.VMEM((angles * x, y), BF)],
        input_output_aliases=aliases,
        compiler_params=params(14),
        cost_estimate=cost(weights.shape[1] * angles * planes * x * y // 4, 3 << 20),
        name="finish",
    )(*operands)


def slant_matrix_of(slant_taper, band_offsets, offset_count):
    offset_index = jnp.arange(offset_count, dtype=jnp.int32)
    depth_shift = jnp.floor_divide(band_offsets[:, None] * offset_index[None, :], offset_count)
    reach_index = jnp.arange(slant_taper.shape[2], dtype=jnp.int32) - R
    inside_band = jnp.abs(reach_index[None, None, :] - depth_shift[:, :, None]) <= BAND
    return jnp.where(inside_band, slant_taper, jnp.zeros_like(slant_taper))


def exchange(x_up, x_down, axis):
    count = lax.axis_size(axis)
    up = [(i, i + 1) for i in range(count - 1)]
    down = [(j, i) for i, j in up]
    return lax.ppermute(x_up, axis, up), lax.ppermute(x_down, axis, down)


def near_of(x, axis):
    count = lax.axis_size(axis)
    return lax.ppermute(x, axis, [(i, i ^ 1) for i in range(count)])


def far_of(x, axis):
    pairs = [(i, i + 1) for i in range(1, lax.axis_size(axis) - 1, 2)]
    return lax.ppermute(x, axis, pairs + [(j, i) for i, j in pairs])


def local(offset_image, dip_class, slant_taper, band_offsets, coefficients):
    h, z, x, y = offset_image.shape
    angles = slant_taper.shape[0]
    before, after = reach_tables(h, R)
    up_a, down_a = exchange(*pack(offset_image, before, after), "depth")
    slant = jnp.transpose(slant_matrix_of(slant_taper, band_offsets, h), (2, 0, 1))
    prepared = prepare(offset_image, coefficients, dip_class, slant, before, after)
    up_b, down_b, mid_a, mid_b, matrix, weights = prepared
    up_b, down_b = exchange(up_b, down_b, "depth")
    (own_a,) = gather(matrix, up_a, down_a, mid_a, before, after, (z,))
    far_a = far_of(own_a, "gx")
    near_a = near_of(own_a, "gx")
    own_b, *parts = gather(matrix, up_b, down_b, mid_b, before, after, LAST_PARTS)
    fars = []
    for part in parts:
        fars.append(far_of(part, "gx"))
    near_b = near_of(own_b, "gx")
    odd = (lax.axis_index("gx") % 2).astype(jnp.int32).reshape(1)
    totals = early(odd, weights, own_a, near_a, None, 0, angles, z, x, y)
    totals = early(odd, weights, own_b, near_b, totals, 1, angles, z, x, y)
    totals = add_far(1 - odd, weights, far_a, totals, angles, z, x, y)
    done, first = None, 0
    for far, planes in zip(fars, LAST_PARTS):
        done = finish(1 - odd, weights, totals, far, done, first, (angles, z, x, y))
        first += planes
    return done


def solution(mesh):
    return jax.shard_map(
        local,
        mesh=mesh,
        in_specs=(P(None, "depth", "gx", None), P("depth", "gx", None), P(), P(), P()),
        out_specs=P(None, "depth", "gx", None),
        check_vma=False,
    )
```

```python
import functools

import jax
import jax.numpy as jnp
from jax import lax
from jax.experimental import pallas as pl
from jax.experimental.pallas import tpu as pltpu
from jax.sharding import PartitionSpec as P


R = 16
BAND = 2
RX = 4
RY = 1
REACH = R - BAND
ZB = 4
HALVES = 2
LAST_PARTS = (8, 4, 4)
PART = 32
SIDES = 2 * RY + 1
BF = jnp.bfloat16
F32 = jnp.float32


def reach_tables(offsets, steps):
    before, after = [], []
    for k in range(1, steps + 1):
        low = [h for h in range(offsets) if -((-REACH * h) // offsets) + BAND >= k]
        high = [h for h in range(offsets) if (REACH * h) // offsets + BAND >= k]
        if low:
            before.append(low[0])
        if high:
            after.append(high[0])
    return before, after


def segments(firsts, offsets):
    out, at = [], 0
    for first in firsts:
        out.append((at, offsets - first))
        at += offsets - first
    return out, at


def spec():
    return pl.BlockSpec(memory_space=pltpu.VMEM)


def params(mib):
    return pltpu.CompilerParams(vmem_limit_bytes=mib << 20)


def cost(flops, moved):
    return pl.CostEstimate(flops=flops, bytes_accessed=moved, transcendentals=0)


def struct(shape, kind=BF):
    return jax.ShapeDtypeStruct(shape, kind)


def swap_matrix(offsets, columns):
    n = offsets * columns
    row = lax.broadcasted_iota(jnp.int32, (n, n), 0)
    col = lax.broadcasted_iota(jnp.int32, (n, n), 1)
    hit = col == (row % offsets) * columns + row // offsets
    return jnp.where(hit, 1.0, 0.0).astype(BF)


def unswap_matrix(angles, columns):
    n = angles * columns
    row = lax.broadcasted_iota(jnp.int32, (n, n), 0)
    col = lax.broadcasted_iota(jnp.int32, (n, n), 1)
    hit = row == (col % angles) * columns + col // angles
    return jnp.where(hit, 1.0, 0.0).astype(BF)


def pack_unit(before, after, image, lanes, columns, up, down):
    h, z = image.shape[:2]
    for k, (at, n) in enumerate(segments(before, h)[0]):
        up[at : at + n] = image[h - n : h, z - 1 - k, columns, lanes]
    for k, (at, n) in enumerate(segments(after, h)[0]):
        down[at : at + n] = image[h - n : h, k, columns, lanes]


def pack_shapes(image, before, after, columns):
    h, _, _, y = image.shape
    n_up, n_down = segments(before, h)[1], segments(after, h)[1]
    return struct((n_up, columns, y // HALVES)), struct((n_down, columns, y // HALVES))


def pack_kernel(before, after, image, up, down, part, sem):
    width = part.shape[3]
    copy = pltpu.make_async_copy(image.at[:, :, :, pl.ds(0, width)], part, sem)
    copy.start()
    copy.wait()
    columns = slice(0, part.shape[2] // 2)
    pack_unit(before, after, part, slice(0, width), columns, up, down)


def pack(image, before, after):
    h, z, x, y = image.shape
    return pl.pallas_call(
        functools.partial(pack_kernel, before, after),
        out_shape=pack_shapes(image, before, after, x // 2),
        in_specs=[pl.BlockSpec(memory_space=pltpu.HBM)],
        out_specs=(spec(),) * 2,
        scratch_shapes=[pltpu.VMEM((h, z, x, y // HALVES), BF), pltpu.SemaphoreType.DMA],
        compiler_params=params(62),
        name="pack",
    )(image)


def prepare_kernel(before, after, image, coefficients, dip, slant, *outs):
    up_a, down_a, up_b, down_b = outs[:4]
    columns, (matrix, weights) = outs[4 : 4 + HALVES], outs[4 + HALVES :]
    h, z, x, y = image.shape
    width = y // HALVES
    pack_unit(before, after, image, slice(0, width), slice(x // 2, x), up_a, down_a)
    pack_unit(before, after, image, slice(width, y), slice(0, x), up_b, down_b)
    swap = swap_matrix(h, x)
    for level in range(z):
        plane = image[:, level].reshape(h * x, y)
        moved = jnp.dot(swap, plane, preferred_element_type=F32).astype(BF)
        for half in range(HALVES):
            for c in range(x):
                at = (c % 2) * width
                columns[half][c // 2, level * h : (level + 1) * h, at : at + width] = moved[
                    c * h : (c + 1) * h, half * width : (half + 1) * width
                ]
    steps, angles, _ = slant.shape
    zero = jnp.zeros((angles, h), BF)
    for j in range(ZB):
        for t in range((steps + ZB - 1) // 2):
            pair = [slant[d] if 0 <= d < steps else zero for d in (2 * t - j, 2 * t + 1 - j)]
            matrix[j * angles : (j + 1) * angles, 2 * t * h : 2 * (t + 1) * h] = jnp.concatenate(
                pair, axis=1
            )
    lane = lax.broadcasted_iota(jnp.int32, (z * x, y), 1)
    classes = dip[...]
    tests = [classes == q for q in range(1, coefficients.shape[0])]
    for t in range(weights.shape[1]):
        w = jnp.full((z * x, y), coefficients[0, t], F32)
        for q, test in enumerate(tests):
            w = jnp.where(test, coefficients[q + 1, t], w)
        shift = t % SIDES - RY
        if shift:
            w = pltpu.roll(w, shift % y, 1)
            w = jnp.where(lane < shift if shift > 0 else lane >= y + shift, 0.0, w)
        for half in range(HALVES):
            weights[half, t] = w[:, half * width : (half + 1) * width]


def prepare(image, coefficients, dip, slant, before, after):
    h, z, x, y = image.shape
    steps, angles, _ = slant.shape
    taps = coefficients.shape[1]
    return pl.pallas_call(
        functools.partial(prepare_kernel, before, after),
        out_shape=(
            *pack_shapes(image, before, after, x // 2),
            *pack_shapes(image, before, after, x),
            *(struct((x // 2, z * h, 2 * y // HALVES)) for _ in range(HALVES)),
            struct((ZB * angles, (steps + ZB - 1) * h)),
            struct((HALVES, taps, z * x, y // HALVES), F32),
        ),
        in_specs=[spec(), pl.BlockSpec(memory_space=pltpu.SMEM), spec(), spec()],
        out_specs=(spec(),) * (6 + HALVES),
        compiler_params=params(14),
        cost_estimate=cost(2 * h * x * h * x * y * z, 8 << 20),
        name="prepare",
    )(image, coefficients, dip.reshape(z * x, y), slant)


def unpack(swap, source, pieces, starts, target):
    h, x = swap.shape[0] // source.shape[1], source.shape[1]
    width = source.shape[2]
    for k in range(0, len(pieces), 2):
        pair = [pieces[min(i, len(pieces) - 1)] for i in (k, k + 1)]
        planes = [source[at + n - h : at + n].reshape(h * x, width) for at, n in pair]
        moved = jnp.dot(swap, jnp.concatenate(planes, axis=1), preferred_element_type=F32)
        moved = moved.astype(BF)
        for i in range(min(2, len(pieces) - k)):
            rows = slice(starts[k + i] * h, (starts[k + i] + 1) * h)
            for c in range(x):
                at = (c % 2) * width
                target[c // 2, rows, at : at + width] = moved[
                    c * h : (c + 1) * h, i * width : (i + 1) * width
                ]


def gather_kernel(before, after, parts, first_pair, matrix, up, down, mid, *rest):
    rest, (low, high) = rest[:-2], rest[-2:]
    given, (own, *outs) = (rest[0], rest[1:]) if first_pair else (None, rest)
    x = up.shape[1]
    m = matrix.shape[0]
    h = matrix.shape[1] // (2 * R + ZB)
    tile = ZB * h
    swap = swap_matrix(h, x)
    unpack(swap, up, segments(before, h)[0], [R - 1 - k for k in range(R)], low)
    unpack(swap, down, segments(after, h)[0], list(range(R)), high)
    for k in range(len(after), R):
        high[:, k * h : (k + 1) * h, :] = jnp.zeros((x // 2, h, high.shape[2]), BF)
    if given is not None:
        own[: 2 * first_pair] = given[...]
    zb = 0
    n_mid = mid.shape[1]
    for index, planes in enumerate(parts):
        for block in range(planes // ZB):
            n_low = low.shape[1] - zb * tile
            n_high = (zb + 1) * tile
            for c in range(x // 2):
                total = jnp.dot(
                    matrix[:, n_low : n_low + n_mid], mid[first_pair + c], preferred_element_type=F32
                )
                total += jnp.dot(
                    matrix[:, :n_low], low[c, zb * tile :, :], preferred_element_type=F32
                )
                total += jnp.dot(
                    matrix[:, n_low + n_mid :], high[c, :n_high, :], preferred_element_type=F32
                )
                moved = total.astype(BF)
                width = moved.shape[1] // 2
                for side in range(2):
                    piece = moved[:, side * width : (side + 1) * width]
                    own[2 * (first_pair + c) + side, zb * m : (zb + 1) * m, :] = piece
                    if outs:
                        outs[index][2 * c + side, block * m : (block + 1) * m, :] = piece
            zb += 1


def gather(matrix, up, down, mid, before, after, parts, given=None):
    rows, width = mid.shape[1:]
    x, z = up.shape[1], sum(parts)
    per_plane = matrix.shape[0] // ZB
    first_pair = 0 if given is None else given.shape[0] // 2
    shapes = [(2 * first_pair + x, z)]
    if len(parts) > 1 or first_pair:
        shapes += [(x, n) for n in parts]
    operands = [matrix, up, down, mid] + ([] if given is None else [given])
    return pl.pallas_call(
        functools.partial(gather_kernel, before, after, parts, first_pair),
        out_shape=tuple(struct((n, planes * per_plane, width // 2)) for n, planes in shapes),
        in_specs=[spec()] * len(operands),
        out_specs=(spec(),) * len(shapes),
        scratch_shapes=[pltpu.VMEM((x // 2, rows, width), BF)] * 2,
        compiler_params=params(14),
        cost_estimate=cost(z * per_plane * matrix.shape[1] * x * width, 6 << 20),
        name="gather",
    )(*operands)


def by_parity(flip_ref, body):
    for value in range(2):
        pl.when(flip_ref[0] == value)(functools.partial(body, value))


def half_sums(weights, half, row, at, terms):
    sums = [None] * SIDES
    for source, c, step in terms:
        values = source[c, pl.ds(at, PART), :].astype(F32)
        for side in range(SIDES):
            w = weights[half, step * SIDES + side, pl.ds(row, 1), :]
            term = w * values
            sums[side] = term if sums[side] is None else sums[side] + term
    return sums


def spread(sums, half):
    zero = jnp.zeros_like(sums[0])
    total = None
    for side in range(SIDES):
        both = jnp.concatenate([sums[side], zero] if half == 0 else [zero, sums[side]], axis=1)
        if side != RY:
            both = pltpu.roll(both, (RY - side) % both.shape[1], 1)
        total = both if total is None else total + both
    return total


def beside_terms(sources, column, x, flip):
    terms = []
    for c in range(x):
        step = c - column + 2 * RX * (1 - flip)
        if 0 <= step <= 2 * RX:
            source = sources[c * len(sources) // x]
            terms.append((source, c % source.shape[0], step))
    return terms


def early_kernel(half, angles, x, flip_ref, weights, own, near, *rest):
    totals = rest[-1]

    def level(flip, j, carry):
        for column in range(x):
            row = j * x + column
            terms = [(own, c, c - column + RX) for c in range(x)]
            terms += beside_terms((near,), column, x, flip)
            for piece in range(angles // PART):
                at = pl.multiple_of(j * angles + piece * PART, PART)
                part = slice(piece * PART, (piece + 1) * PART)
                total = spread(half_sums(weights, half, row, at, terms), half)
                if len(rest) > 1:
                    total = total + rest[0][row, part, :]
                totals[row, part, :] = total
        return carry

    def run(flip):
        lax.fori_loop(0, totals.shape[0] // x, functools.partial(level, flip), 0)

    by_parity(flip_ref, run)


def scalar_spec():
    return pl.BlockSpec(memory_space=pltpu.SMEM)


def early(flip, weights, own, near, totals, half, angles, z, x, y):
    operands = [flip, weights, own, near] + ([] if totals is None else [totals])
    return pl.pallas_call(
        functools.partial(early_kernel, half, angles, x),
        out_shape=struct((z * x, angles, y), F32),
        in_specs=[scalar_spec()] + [spec()] * (len(operands) - 1),
        out_specs=spec(),
        compiler_params=params(14),
        cost_estimate=cost(weights.shape[1] * angles * z * x * y, 10 << 20),
        name="early",
    )(*operands)


def add_far_kernel(angles, x, flip_ref, weights, far_1, far_2, given, totals):
    def level(flip, j, carry):
        for column in range(x):
            row = j * x + column
            terms = beside_terms((far_1, far_2), column, x, flip)
            for piece in range(angles // PART):
                at = pl.multiple_of(j * angles + piece * PART, PART)
                part = slice(piece * PART, (piece + 1) * PART)
                sums = half_sums(weights, 0, row, at, terms)
                totals[row, part, :] = given[row, part, :] + spread(sums, 0)
        return carry

    def run(flip):
        lax.fori_loop(0, totals.shape[0] // x, functools.partial(level, flip), 0)

    by_parity(flip_ref, run)


def add_far(flip, weights, far_1, far_2, totals, angles, z, x, y):
    return pl.pallas_call(
        functools.partial(add_far_kernel, angles, x),
        out_shape=struct((z * x, angles, y), F32),
        in_specs=[scalar_spec()] + [spec()] * 4,
        out_specs=spec(),
        compiler_params=params(14),
        cost_estimate=cost(weights.shape[1] * angles * z * x * y // 4, 8 << 20),
        name="add_far",
    )(flip, weights, far_1, far_2, totals)


def finish_kernel(angles, x, first, flip_ref, weights, totals, far, *rest):
    out, scratch = rest[-2:]
    unswap = unswap_matrix(angles, x)
    base = pl.program_id(0) * ZB

    def level(flip, j, carry):
        for column in range(x):
            row = (first + base + j) * x + column
            terms = beside_terms((far,), column, x, flip)
            for piece in range(angles // PART):
                at = pl.multiple_of((base + j) * angles + piece * PART, PART)
                part = slice(piece * PART, (piece + 1) * PART)
                sums = half_sums(weights, 1, row, at, terms)
                total = totals[row, part, :] + spread(sums, 1)
                to = column * angles + piece * PART
                scratch[to : to + PART, :] = total.astype(BF)
        moved = jnp.dot(unswap, scratch[...], preferred_element_type=F32)
        out[:, j] = moved.astype(BF).reshape(angles, x, out.shape[3])
        return carry

    def run(flip):
        lax.fori_loop(0, ZB, functools.partial(level, flip), 0)

    by_parity(flip_ref, run)


def finish(flip, weights, totals, far, done, first, shape):
    angles, _, x, y = shape
    planes = far.shape[1] // angles
    in_specs = [scalar_spec()] + [spec()] * 3
    operands = [flip, weights, totals, far]
    aliases = {}
    if done is not None:
        in_specs.append(pl.BlockSpec(memory_space=pl.ANY))
        operands.append(done)
        aliases = {4: 0}
    return pl.pallas_call(
        functools.partial(finish_kernel, angles, x, first),
        grid=(planes // ZB,),
        out_shape=struct(shape),
        in_specs=in_specs,
        out_specs=pl.BlockSpec((angles, ZB, x, y), lambda i: (0, first // ZB + i, 0, 0)),
        scratch_shapes=[pltpu.VMEM((angles * x, y), BF)],
        input_output_aliases=aliases,
        compiler_params=params(14),
        cost_estimate=cost(weights.shape[1] * angles * planes * x * y // 4, 3 << 20),
        name="finish",
    )(*operands)


def slant_matrix_of(slant_taper, band_offsets, offset_count):
    offset_index = jnp.arange(offset_count, dtype=jnp.int32)
    depth_shift = jnp.floor_divide(band_offsets[:, None] * offset_index[None, :], offset_count)
    reach_index = jnp.arange(slant_taper.shape[2], dtype=jnp.int32) - R
    inside_band = jnp.abs(reach_index[None, None, :] - depth_shift[:, :, None]) <= BAND
    return jnp.where(inside_band, slant_taper, jnp.zeros_like(slant_taper))


def exchange(x_up, x_down, axis):
    count = lax.axis_size(axis)
    up = [(i, i + 1) for i in range(count - 1)]
    down = [(j, i) for i, j in up]
    from_up = lax.ppermute(x_up, axis, up)
    from_down = lax.ppermute(x_down, axis, down)
    return from_up, from_down


def near_of(x, axis):
    count = lax.axis_size(axis)
    return lax.ppermute(x, axis, [(i, i ^ 1) for i in range(count)])


def far_of(x, axis):
    pairs = [(i, i + 1) for i in range(1, lax.axis_size(axis) - 1, 2)]
    return lax.ppermute(x, axis, pairs + [(j, i) for i, j in pairs])


def local(offset_image, dip_class, slant_taper, band_offsets, coefficients):
    h, z, x, y = offset_image.shape
    angles = slant_taper.shape[0]
    before, after = reach_tables(h, R)
    halo_1 = exchange(*pack(offset_image, before, after), "depth")
    slant = jnp.transpose(slant_matrix_of(slant_taper, band_offsets, h), (2, 0, 1))
    prepared = prepare(offset_image, coefficients, dip_class, slant, before, after)
    mid_a, mid_b, matrix, weights = prepared[4:]
    halo_2 = exchange(*prepared[:2], "depth")
    halo_b = exchange(*prepared[2:4], "depth")
    (own_1,) = gather(matrix, *halo_1, mid_a, before, after, (z,))
    far_1 = far_of(own_1, "gx")
    own_a, own_2 = gather(matrix, *halo_2, mid_a, before, after, (z,), own_1)
    far_2 = far_of(own_2, "gx")
    near_a = near_of(own_a, "gx")
    own_b, *parts = gather(matrix, *halo_b, mid_b, before, after, LAST_PARTS)
    fars = []
    for part in parts:
        fars.append(far_of(part, "gx"))
    near_b = near_of(own_b, "gx")
    odd = (lax.axis_index("gx") % 2).astype(jnp.int32).reshape(1)
    totals = early(odd, weights, own_a, near_a, None, 0, angles, z, x, y)
    totals = early(odd, weights, own_b, near_b, totals, 1, angles, z, x, y)
    totals = add_far(1 - odd, weights, far_1, far_2, totals, angles, z, x, y)
    done, first = None, 0
    for far, planes in zip(fars, LAST_PARTS):
        done = finish(1 - odd, weights, totals, far, done, first, (angles, z, x, y))
        first += planes
    return done


def solution(mesh):
    return jax.shard_map(
        local,
        mesh=mesh,
        in_specs=(P(None, "depth", "gx", None), P("depth", "gx", None), P(), P(), P()),
        out_specs=P(None, "depth", "gx", None),
        check_vma=False,
    )
```

```python
import functools

import jax
import jax.numpy as jnp
from jax import lax
from jax.experimental import pallas as pl
from jax.experimental.pallas import tpu as pltpu
from jax.sharding import PartitionSpec as P


R = 16
BAND = 2
RX = 4
RY = 1
REACH = R - BAND
ZB = 4
HALVES = 2
LAST_PARTS = (8, 8)
PART = 32
SIDES = 2 * RY + 1
BF = jnp.bfloat16
F32 = jnp.float32


def reach_tables(offsets, steps):
    before, after = [], []
    for k in range(1, steps + 1):
        low = [h for h in range(offsets) if -((-REACH * h) // offsets) + BAND >= k]
        high = [h for h in range(offsets) if (REACH * h) // offsets + BAND >= k]
        if low:
            before.append(low[0])
        if high:
            after.append(high[0])
    return before, after


def segments(firsts, offsets):
    out, at = [], 0
    for first in firsts:
        out.append((at, offsets - first))
        at += offsets - first
    return out, at


def spec():
    return pl.BlockSpec(memory_space=pltpu.VMEM)


def params(mib):
    return pltpu.CompilerParams(vmem_limit_bytes=mib << 20)


def cost(flops, moved):
    return pl.CostEstimate(flops=flops, bytes_accessed=moved, transcendentals=0)


def struct(shape, kind=BF):
    return jax.ShapeDtypeStruct(shape, kind)


def swap_matrix(offsets, columns):
    n = offsets * columns
    row = lax.broadcasted_iota(jnp.int32, (n, n), 0)
    col = lax.broadcasted_iota(jnp.int32, (n, n), 1)
    hit = col == (row % offsets) * columns + row // offsets
    return jnp.where(hit, 1.0, 0.0).astype(BF)


def unswap_matrix(angles, columns):
    n = angles * columns
    row = lax.broadcasted_iota(jnp.int32, (n, n), 0)
    col = lax.broadcasted_iota(jnp.int32, (n, n), 1)
    hit = row == (col % angles) * columns + col // angles
    return jnp.where(hit, 1.0, 0.0).astype(BF)


def pack_half(before, after, half, image, up, down):
    h, z = image.shape[:2]
    width = up.shape[2]
    lanes = slice(half * width, (half + 1) * width)
    for k, (at, n) in enumerate(segments(before, h)[0]):
        up[at : at + n] = image[h - n : h, z - 1 - k, :, lanes]
    for k, (at, n) in enumerate(segments(after, h)[0]):
        down[at : at + n] = image[h - n : h, k, :, lanes]


def pack_shapes(image, before, after):
    h, _, x, y = image.shape
    n_up, n_down = segments(before, h)[1], segments(after, h)[1]
    return struct((n_up, x, y // HALVES)), struct((n_down, x, y // HALVES))


def pack_kernel(before, after, image, up, down, part, sem):
    copy = pltpu.make_async_copy(image.at[:, :, :, pl.ds(0, part.shape[3])], part, sem)
    copy.start()
    copy.wait()
    pack_half(before, after, 0, part, up, down)


def pack(image, before, after):
    h, z, x, y = image.shape
    return pl.pallas_call(
        functools.partial(pack_kernel, before, after),
        out_shape=pack_shapes(image, before, after),
        in_specs=[pl.BlockSpec(memory_space=pltpu.HBM)],
        out_specs=(spec(),) * 2,
        scratch_shapes=[pltpu.VMEM((h, z, x, y // HALVES), BF), pltpu.SemaphoreType.DMA],
        compiler_params=params(62),
        name="pack",
    )(image)


def prepare_kernel(before, after, image, coefficients, dip, slant, up, down, *outs):
    columns, (matrix, weights) = outs[:HALVES], outs[HALVES:]
    h, z, x, y = image.shape
    width = y // HALVES
    pack_half(before, after, 1, image, up, down)
    swap = swap_matrix(h, x)
    for level in range(z):
        plane = image[:, level].reshape(h * x, y)
        moved = jnp.dot(swap, plane, preferred_element_type=F32).astype(BF)
        for half in range(HALVES):
            for c in range(x):
                at = (c % 2) * width
                columns[half][c // 2, level * h : (level + 1) * h, at : at + width] = moved[
                    c * h : (c + 1) * h, half * width : (half + 1) * width
                ]
    steps, angles, _ = slant.shape
    zero = jnp.zeros((angles, h), BF)
    for j in range(ZB):
        for t in range((steps + ZB - 1) // 2):
            pair = [slant[d] if 0 <= d < steps else zero for d in (2 * t - j, 2 * t + 1 - j)]
            matrix[j * angles : (j + 1) * angles, 2 * t * h : 2 * (t + 1) * h] = jnp.concatenate(
                pair, axis=1
            )
    lane = lax.broadcasted_iota(jnp.int32, (z * x, y), 1)
    classes = dip[...]
    tests = [classes == q for q in range(1, coefficients.shape[0])]
    for t in range(weights.shape[1]):
        w = jnp.full((z * x, y), coefficients[0, t], F32)
        for q, test in enumerate(tests):
            w = jnp.where(test, coefficients[q + 1, t], w)
        shift = t % SIDES - RY
        if shift:
            w = pltpu.roll(w, shift % y, 1)
            w = jnp.where(lane < shift if shift > 0 else lane >= y + shift, 0.0, w)
        for half in range(HALVES):
            weights[half, t] = w[:, half * width : (half + 1) * width]


def prepare(image, coefficients, dip, slant, before, after):
    h, z, x, y = image.shape
    steps, angles, _ = slant.shape
    taps = coefficients.shape[1]
    return pl.pallas_call(
        functools.partial(prepare_kernel, before, after),
        out_shape=(
            *pack_shapes(image, before, after),
            *(struct((x // 2, z * h, 2 * y // HALVES)) for _ in range(HALVES)),
            struct((ZB * angles, (steps + ZB - 1) * h)),
            struct((HALVES, taps, z * x, y // HALVES), F32),
        ),
        in_specs=[spec(), pl.BlockSpec(memory_space=pltpu.SMEM), spec(), spec()],
        out_specs=(spec(),) * (4 + HALVES),
        compiler_params=params(14),
        cost_estimate=cost(2 * h * x * h * x * y * z, 8 << 20),
        name="prepare",
    )(image, coefficients, dip.reshape(z * x, y), slant)


def unpack(swap, source, pieces, starts, target):
    h, x = swap.shape[0] // source.shape[1], source.shape[1]
    width = source.shape[2]
    for k in range(0, len(pieces), 2):
        pair = [pieces[min(i, len(pieces) - 1)] for i in (k, k + 1)]
        planes = [source[at + n - h : at + n].reshape(h * x, width) for at, n in pair]
        moved = jnp.dot(swap, jnp.concatenate(planes, axis=1), preferred_element_type=F32)
        moved = moved.astype(BF)
        for i in range(min(2, len(pieces) - k)):
            rows = slice(starts[k + i] * h, (starts[k + i] + 1) * h)
            for c in range(x):
                at = (c % 2) * width
                target[c // 2, rows, at : at + width] = moved[
                    c * h : (c + 1) * h, i * width : (i + 1) * width
                ]


def partial_kernel(matrix, mid_a, mid_b, out_a, out_b):
    h = matrix.shape[1] // (2 * R + ZB)
    for mid, out in ((mid_a, out_a), (mid_b, out_b)):
        n_mid = mid.shape[1]
        for zb in range(out.shape[0]):
            n_low = n_mid - zb * ZB * h
            for c in range(mid.shape[0]):
                out[zb, c] = jnp.dot(
                    matrix[:, n_low : n_low + n_mid], mid[c], preferred_element_type=F32
                )


def own_part(matrix, mid_a, mid_b, z):
    pairs, rows, width = mid_a.shape
    m = matrix.shape[0]
    return pl.pallas_call(
        partial_kernel,
        out_shape=(struct((z // ZB, pairs, m, width), F32),) * 2,
        in_specs=[spec()] * 3,
        out_specs=(spec(),) * 2,
        compiler_params=params(14),
        cost_estimate=cost(4 * (z // ZB) * m * rows * pairs * width, 9 << 20),
        name="own_part",
    )(matrix, mid_a, mid_b)


def gather_kernel(before, after, parts, matrix, up, down, given, *rest):
    (own, *outs), (low, high) = rest[:-2], rest[-2:]
    x = up.shape[1]
    m = matrix.shape[0]
    h = matrix.shape[1] // (2 * R + ZB)
    tile = ZB * h
    swap = swap_matrix(h, x)
    unpack(swap, up, segments(before, h)[0], [R - 1 - k for k in range(R)], low)
    unpack(swap, down, segments(after, h)[0], list(range(R)), high)
    for k in range(len(after), R):
        high[:, k * h : (k + 1) * h, :] = jnp.zeros((x // 2, h, high.shape[2]), BF)
    zb = 0
    n_mid = matrix.shape[1] - ZB * h - low.shape[1]
    for index, planes in enumerate(parts):
        for block in range(planes // ZB):
            n_low = low.shape[1] - zb * tile
            n_high = (zb + 1) * tile
            for c in range(x // 2):
                total = given[zb, c] + jnp.dot(
                    matrix[:, :n_low], low[c, zb * tile :, :], preferred_element_type=F32
                )
                total += jnp.dot(
                    matrix[:, n_low + n_mid :], high[c, :n_high, :], preferred_element_type=F32
                )
                moved = total.astype(BF)
                width = moved.shape[1] // 2
                for side in range(2):
                    piece = moved[:, side * width : (side + 1) * width]
                    own[2 * c + side, zb * m : (zb + 1) * m, :] = piece
                    if outs:
                        outs[index][2 * c + side, block * m : (block + 1) * m, :] = piece
            zb += 1


def gather(matrix, up, down, given, before, after, parts):
    _, pairs, _, width = given.shape
    rows = sum(parts) * (matrix.shape[1] // (2 * R + ZB))
    per_plane = matrix.shape[0] // ZB
    sizes = (sum(parts), *(parts if len(parts) > 1 else ()))
    return pl.pallas_call(
        functools.partial(gather_kernel, before, after, parts),
        out_shape=tuple(struct((2 * pairs, n * per_plane, width // 2)) for n in sizes),
        in_specs=[spec()] * 4,
        out_specs=(spec(),) * len(sizes),
        scratch_shapes=[pltpu.VMEM((pairs, rows, width), BF)] * 2,
        compiler_params=params(14),
        cost_estimate=cost(2 * sum(parts) * per_plane * matrix.shape[1] * pairs * width, 6 << 20),
        name="gather",
    )(matrix, up, down, given)


def mirrored(n, count, flip):
    return n + flip * (count - 1 - 2 * n)


def half_sums(weights, half, row, at, terms):
    sums = [None] * SIDES
    for source, c, step in terms:
        values = source[c, pl.ds(at, PART), :].astype(F32)
        for side in range(SIDES):
            w = weights[half, step * SIDES + side, pl.ds(row, 1), :]
            term = w * values
            sums[side] = term if sums[side] is None else sums[side] + term
    return sums


def spread(sums, half):
    zero = jnp.zeros_like(sums[0])
    total = None
    for side in range(SIDES):
        both = jnp.concatenate([sums[side], zero] if half == 0 else [zero, sums[side]], axis=1)
        if side != RY:
            both = pltpu.roll(both, (RY - side) % both.shape[1], 1)
        total = both if total is None else total + both
    return total


def beside_terms(source, n, column, x, flip):
    terms = []
    for m in range(n + 1):
        c = mirrored(m, x, flip)
        terms.append((source, c, c - column + 2 * RX * (1 - flip)))
    return terms


def early_kernel(half, angles, x, flip_ref, weights, own, near, *rest):
    totals = rest[-1]
    flip = flip_ref[0]

    def level(j, carry):
        for n in range(x):
            column = mirrored(n, x, flip)
            row = j * x + column
            terms = [(own, c, c - column + RX) for c in range(x)]
            terms += beside_terms(near, n, column, x, flip)
            for piece in range(angles // PART):
                at = pl.multiple_of(j * angles + piece * PART, PART)
                part = slice(piece * PART, (piece + 1) * PART)
                total = spread(half_sums(weights, half, row, at, terms), half)
                if len(rest) > 1:
                    total = total + rest[0][row, part, :]
                totals[row, part, :] = total
        return carry

    lax.fori_loop(0, totals.shape[0] // x, level, 0)


def scalar_spec():
    return pl.BlockSpec(memory_space=pltpu.SMEM)


def early(flip, weights, own, near, totals, half, angles, z, x, y):
    operands = [flip, weights, own, near] + ([] if totals is None else [totals])
    return pl.pallas_call(
        functools.partial(early_kernel, half, angles, x),
        out_shape=struct((z * x, angles, y), F32),
        in_specs=[scalar_spec()] + [spec()] * (len(operands) - 1),
        out_specs=spec(),
        compiler_params=params(14),
        cost_estimate=cost(weights.shape[1] * angles * z * x * y, 10 << 20),
        name="early",
    )(*operands)


def add_far_kernel(angles, x, flip_ref, weights, far, given, totals):
    flip = flip_ref[0]

    def level(j, carry):
        for n in range(x):
            column = mirrored(n, x, flip)
            row = j * x + column
            terms = beside_terms(far, n, column, x, flip)
            for piece in range(angles // PART):
                at = pl.multiple_of(j * angles + piece * PART, PART)
                part = slice(piece * PART, (piece + 1) * PART)
                sums = half_sums(weights, 0, row, at, terms)
                totals[row, part, :] = given[row, part, :] + spread(sums, 0)
        return carry

    lax.fori_loop(0, totals.shape[0] // x, level, 0)


def add_far(flip, weights, far, totals, angles, z, x, y):
    return pl.pallas_call(
        functools.partial(add_far_kernel, angles, x),
        out_shape=struct((z * x, angles, y), F32),
        in_specs=[scalar_spec()] + [spec()] * 3,
        out_specs=spec(),
        compiler_params=params(14),
        cost_estimate=cost(weights.shape[1] * angles * z * x * y // 4, 8 << 20),
        name="add_far",
    )(flip, weights, far, totals)


def finish_kernel(angles, x, first, flip_ref, weights, totals, far, *rest):
    out, scratch = rest[-2:]
    flip = flip_ref[0]
    unswap = unswap_matrix(angles, x)
    base = pl.program_id(0) * ZB

    def level(j, carry):
        for n in range(x):
            column = mirrored(n, x, flip)
            row = (first + base + j) * x + column
            terms = beside_terms(far, n, column, x, flip)
            for piece in range(angles // PART):
                at = pl.multiple_of((base + j) * angles + piece * PART, PART)
                part = slice(piece * PART, (piece + 1) * PART)
                sums = half_sums(weights, 1, row, at, terms)
                total = totals[row, part, :] + spread(sums, 1)
                to = pl.multiple_of(column * angles + piece * PART, PART)
                scratch[pl.ds(to, PART), :] = total.astype(BF)
        moved = jnp.dot(unswap, scratch[...], preferred_element_type=F32)
        out[:, j] = moved.astype(BF).reshape(angles, x, out.shape[3])
        return carry

    lax.fori_loop(0, ZB, level, 0)


def finish(flip, weights, totals, far, done, first, shape):
    angles, _, x, y = shape
    planes = far.shape[1] // angles
    in_specs = [scalar_spec()] + [spec()] * 3
    operands = [flip, weights, totals, far]
    aliases = {}
    if done is not None:
        in_specs.append(pl.BlockSpec(memory_space=pl.ANY))
        operands.append(done)
        aliases = {4: 0}
    return pl.pallas_call(
        functools.partial(finish_kernel, angles, x, first),
        grid=(planes // ZB,),
        out_shape=struct(shape),
        in_specs=in_specs,
        out_specs=pl.BlockSpec((angles, ZB, x, y), lambda i: (0, first // ZB + i, 0, 0)),
        scratch_shapes=[pltpu.VMEM((angles * x, y), BF)],
        input_output_aliases=aliases,
        compiler_params=params(14),
        cost_estimate=cost(weights.shape[1] * angles * planes * x * y // 4, 3 << 20),
        name="finish",
    )(*operands)


def slant_matrix_of(slant_taper, band_offsets, offset_count):
    offset_index = jnp.arange(offset_count, dtype=jnp.int32)
    depth_shift = jnp.floor_divide(band_offsets[:, None] * offset_index[None, :], offset_count)
    reach_index = jnp.arange(slant_taper.shape[2], dtype=jnp.int32) - R
    inside_band = jnp.abs(reach_index[None, None, :] - depth_shift[:, :, None]) <= BAND
    return jnp.where(inside_band, slant_taper, jnp.zeros_like(slant_taper))


def exchange(x_up, x_down, axis):
    count = lax.axis_size(axis)
    up = [(i, i + 1) for i in range(count - 1)]
    down = [(j, i) for i, j in up]
    from_up = lax.ppermute(x_up, axis, up)
    from_down = lax.ppermute(x_down, axis, down)
    return from_up, from_down


def near_of(x, axis):
    count = lax.axis_size(axis)
    return lax.ppermute(x, axis, [(i, i ^ 1) for i in range(count)])


def far_of(x, axis):
    pairs = [(i, i + 1) for i in range(1, lax.axis_size(axis) - 1, 2)]
    return lax.ppermute(x, axis, pairs + [(j, i) for i, j in pairs])


def local(offset_image, dip_class, slant_taper, band_offsets, coefficients):
    h, z, x, y = offset_image.shape
    angles = slant_taper.shape[0]
    before, after = reach_tables(h, R)
    up_a, down_a = exchange(*pack(offset_image, before, after), "depth")
    slant = jnp.transpose(slant_matrix_of(slant_taper, band_offsets, h), (2, 0, 1))
    prepared = prepare(offset_image, coefficients, dip_class, slant, before, after)
    up_b, down_b, mid_a, mid_b, matrix, weights = prepared
    up_b, down_b = exchange(up_b, down_b, "depth")
    part_a, part_b = own_part(matrix, mid_a, mid_b, z)
    (own_a,) = gather(matrix, up_a, down_a, part_a, before, after, (z,))
    far_a = far_of(own_a, "gx")
    near_a = near_of(own_a, "gx")
    own_b, *parts = gather(matrix, up_b, down_b, part_b, before, after, LAST_PARTS)
    fars = []
    for part in parts:
        fars.append(far_of(part, "gx"))
    near_b = near_of(own_b, "gx")
    odd = (lax.axis_index("gx") % 2).astype(jnp.int32).reshape(1)
    totals = early(odd, weights, own_a, near_a, None, 0, angles, z, x, y)
    totals = early(odd, weights, own_b, near_b, totals, 1, angles, z, x, y)
    totals = add_far(1 - odd, weights, far_a, totals, angles, z, x, y)
    done, first = None, 0
    for far, planes in zip(fars, LAST_PARTS):
        done = finish(1 - odd, weights, totals, far, done, first, (angles, z, x, y))
        first += planes
    return done


def solution(mesh):
    return jax.shard_map(
        local,
        mesh=mesh,
        in_specs=(P(None, "depth", "gx", None), P("depth", "gx", None), P(), P(), P()),
        out_specs=P(None, "depth", "gx", None),
        check_vma=False,
    )
```

```python
import functools

import jax
import jax.numpy as jnp
from jax import lax
from jax.experimental import pallas as pl
from jax.experimental.pallas import tpu as pltpu
from jax.sharding import PartitionSpec as P


R = 16
BAND = 2
RX = 4
RY = 1
REACH = R - BAND
ZB = 4
HALVES = 2
LAST_PARTS = (8, 4, 4)
PART = 32
SIDES = 2 * RY + 1
BF = jnp.bfloat16
F32 = jnp.float32


def reach_tables(offsets, steps):
    before, after = [], []
    for k in range(1, steps + 1):
        low = [h for h in range(offsets) if -((-REACH * h) // offsets) + BAND >= k]
        high = [h for h in range(offsets) if (REACH * h) // offsets + BAND >= k]
        if low:
            before.append(low[0])
        if high:
            after.append(high[0])
    return before, after


def segments(firsts, offsets):
    out, at = [], 0
    for first in firsts:
        out.append((at, offsets - first))
        at += offsets - first
    return out, at


def spec():
    return pl.BlockSpec(memory_space=pltpu.VMEM)


def params(mib):
    return pltpu.CompilerParams(vmem_limit_bytes=mib << 20)


def cost(flops, moved):
    return pl.CostEstimate(flops=flops, bytes_accessed=moved, transcendentals=0)


def struct(shape, kind=BF):
    return jax.ShapeDtypeStruct(shape, kind)


def swap_matrix(offsets, columns):
    n = offsets * columns
    row = lax.broadcasted_iota(jnp.int32, (n, n), 0)
    col = lax.broadcasted_iota(jnp.int32, (n, n), 1)
    hit = col == (row % offsets) * columns + row // offsets
    return jnp.where(hit, 1.0, 0.0).astype(BF)


def unswap_matrix(angles, columns):
    n = angles * columns
    row = lax.broadcasted_iota(jnp.int32, (n, n), 0)
    col = lax.broadcasted_iota(jnp.int32, (n, n), 1)
    hit = row == (col % angles) * columns + col // angles
    return jnp.where(hit, 1.0, 0.0).astype(BF)


def pack_half(before, after, half, image, up, down):
    h, z = image.shape[:2]
    width = up.shape[2]
    lanes = slice(half * width, (half + 1) * width)
    for k, (at, n) in enumerate(segments(before, h)[0]):
        up[at : at + n] = image[h - n : h, z - 1 - k, :, lanes]
    for k, (at, n) in enumerate(segments(after, h)[0]):
        down[at : at + n] = image[h - n : h, k, :, lanes]


def pack_shapes(image, before, after):
    h, _, x, y = image.shape
    n_up, n_down = segments(before, h)[1], segments(after, h)[1]
    return struct((n_up, x, y // HALVES)), struct((n_down, x, y // HALVES))


def pack_kernel(before, after, image, up, down, part, sem):
    copy = pltpu.make_async_copy(image.at[:, :, :, pl.ds(0, part.shape[3])], part, sem)
    copy.start()
    copy.wait()
    pack_half(before, after, 0, part, up, down)


def pack(image, before, after):
    h, z, x, y = image.shape
    return pl.pallas_call(
        functools.partial(pack_kernel, before, after),
        out_shape=pack_shapes(image, before, after),
        in_specs=[pl.BlockSpec(memory_space=pltpu.HBM)],
        out_specs=(spec(),) * 2,
        scratch_shapes=[pltpu.VMEM((h, z, x, y // HALVES), BF), pltpu.SemaphoreType.DMA],
        compiler_params=params(62),
        name="pack",
    )(image)


def prepare_kernel(before, after, image, coefficients, dip, slant, up, down, *outs):
    columns, (matrix, weights) = outs[:HALVES], outs[HALVES:]
    h, z, x, y = image.shape
    width = y // HALVES
    pack_half(before, after, 1, image, up, down)
    swap = swap_matrix(h, x)
    for level in range(z):
        plane = image[:, level].reshape(h * x, y)
        moved = jnp.dot(swap, plane, preferred_element_type=F32).astype(BF)
        for half in range(HALVES):
            for c in range(x):
                at = (c % 2) * width
                columns[half][c // 2, level * h : (level + 1) * h, at : at + width] = moved[
                    c * h : (c + 1) * h, half * width : (half + 1) * width
                ]
    steps, angles, _ = slant.shape
    zero = jnp.zeros((angles, h), BF)
    for j in range(ZB):
        for t in range((steps + ZB - 1) // 2):
            pair = [slant[d] if 0 <= d < steps else zero for d in (2 * t - j, 2 * t + 1 - j)]
            matrix[j * angles : (j + 1) * angles, 2 * t * h : 2 * (t + 1) * h] = jnp.concatenate(
                pair, axis=1
            )
    lane = lax.broadcasted_iota(jnp.int32, (z * x, y), 1)
    classes = dip[...]
    tests = [classes == q for q in range(1, coefficients.shape[0])]
    for t in range(weights.shape[1]):
        w = jnp.full((z * x, y), coefficients[0, t], F32)
        for q, test in enumerate(tests):
            w = jnp.where(test, coefficients[q + 1, t], w)
        shift = t % SIDES - RY
        if shift:
            w = pltpu.roll(w, shift % y, 1)
            w = jnp.where(lane < shift if shift > 0 else lane >= y + shift, 0.0, w)
        for half in range(HALVES):
            weights[half, t] = w[:, half * width : (half + 1) * width]


def prepare(image, coefficients, dip, slant, before, after):
    h, z, x, y = image.shape
    steps, angles, _ = slant.shape
    taps = coefficients.shape[1]
    return pl.pallas_call(
        functools.partial(prepare_kernel, before, after),
        out_shape=(
            *pack_shapes(image, before, after),
            *(struct((x // 2, z * h, 2 * y // HALVES)) for _ in range(HALVES)),
            struct((ZB * angles, (steps + ZB - 1) * h)),
            struct((HALVES, taps, z * x, y // HALVES), F32),
        ),
        in_specs=[spec(), pl.BlockSpec(memory_space=pltpu.SMEM), spec(), spec()],
        out_specs=(spec(),) * (4 + HALVES),
        compiler_params=params(14),
        cost_estimate=cost(2 * h * x * h * x * y * z, 8 << 20),
        name="prepare",
    )(image, coefficients, dip.reshape(z * x, y), slant)


def unpack(swap, source, pieces, starts, target):
    h, x = swap.shape[0] // source.shape[1], source.shape[1]
    width = source.shape[2]
    for k in range(0, len(pieces), 2):
        pair = [pieces[min(i, len(pieces) - 1)] for i in (k, k + 1)]
        planes = [source[at + n - h : at + n].reshape(h * x, width) for at, n in pair]
        moved = jnp.dot(swap, jnp.concatenate(planes, axis=1), preferred_element_type=F32)
        moved = moved.astype(BF)
        for i in range(min(2, len(pieces) - k)):
            rows = slice(starts[k + i] * h, (starts[k + i] + 1) * h)
            for c in range(x):
                at = (c % 2) * width
                target[c // 2, rows, at : at + width] = moved[
                    c * h : (c + 1) * h, i * width : (i + 1) * width
                ]


def partial_kernel(matrix, mid_a, mid_b, out_a, out_b):
    h = matrix.shape[1] // (2 * R + ZB)
    for mid, out in ((mid_a, out_a), (mid_b, out_b)):
        n_mid = mid.shape[1]
        for zb in range(out.shape[0]):
            n_low = n_mid - zb * ZB * h
            for c in range(mid.shape[0]):
                out[zb, c] = jnp.dot(
                    matrix[:, n_low : n_low + n_mid], mid[c], preferred_element_type=F32
                )


def own_part(matrix, mid_a, mid_b, z):
    pairs, rows, width = mid_a.shape
    m = matrix.shape[0]
    return pl.pallas_call(
        partial_kernel,
        out_shape=(struct((z // ZB, pairs, m, width), F32),) * 2,
        in_specs=[spec()] * 3,
        out_specs=(spec(),) * 2,
        compiler_params=params(14),
        cost_estimate=cost(4 * (z // ZB) * m * rows * pairs * width, 9 << 20),
        name="own_part",
    )(matrix, mid_a, mid_b)


def gather_kernel(before, after, parts, matrix, up, down, given, *rest):
    (own, *outs), (low, high) = rest[:-2], rest[-2:]
    x = up.shape[1]
    m = matrix.shape[0]
    h = matrix.shape[1] // (2 * R + ZB)
    tile = ZB * h
    swap = swap_matrix(h, x)
    unpack(swap, up, segments(before, h)[0], [R - 1 - k for k in range(R)], low)
    unpack(swap, down, segments(after, h)[0], list(range(R)), high)
    for k in range(len(after), R):
        high[:, k * h : (k + 1) * h, :] = jnp.zeros((x // 2, h, high.shape[2]), BF)
    zb = 0
    n_mid = matrix.shape[1] - ZB * h - low.shape[1]
    for index, planes in enumerate(parts):
        for block in range(planes // ZB):
            n_low = low.shape[1] - zb * tile
            n_high = (zb + 1) * tile
            for c in range(x // 2):
                total = given[zb, c] + jnp.dot(
                    matrix[:, :n_low], low[c, zb * tile :, :], preferred_element_type=F32
                )
                total += jnp.dot(
                    matrix[:, n_low + n_mid :], high[c, :n_high, :], preferred_element_type=F32
                )
                moved = total.astype(BF)
                width = moved.shape[1] // 2
                for side in range(2):
                    piece = moved[:, side * width : (side + 1) * width]
                    own[2 * c + side, zb * m : (zb + 1) * m, :] = piece
                    if outs:
                        outs[index][2 * c + side, block * m : (block + 1) * m, :] = piece
            zb += 1


def gather(matrix, up, down, given, before, after, parts):
    _, pairs, _, width = given.shape
    rows = sum(parts) * (matrix.shape[1] // (2 * R + ZB))
    per_plane = matrix.shape[0] // ZB
    sizes = (sum(parts), *(parts if len(parts) > 1 else ()))
    return pl.pallas_call(
        functools.partial(gather_kernel, before, after, parts),
        out_shape=tuple(struct((2 * pairs, n * per_plane, width // 2)) for n in sizes),
        in_specs=[spec()] * 4,
        out_specs=(spec(),) * len(sizes),
        scratch_shapes=[pltpu.VMEM((pairs, rows, width), BF)] * 2,
        compiler_params=params(14),
        cost_estimate=cost(2 * sum(parts) * per_plane * matrix.shape[1] * pairs * width, 6 << 20),
        name="gather",
    )(matrix, up, down, given)


def mirrored(n, count, flip):
    return n + flip * (count - 1 - 2 * n)


def half_sums(weights, half, row, at, terms):
    sums = [None] * SIDES
    for source, c, step in terms:
        values = source[c, pl.ds(at, PART), :].astype(F32)
        for side in range(SIDES):
            w = weights[half, step * SIDES + side, pl.ds(row, 1), :]
            term = w * values
            sums[side] = term if sums[side] is None else sums[side] + term
    return sums


def spread(sums, half):
    zero = jnp.zeros_like(sums[0])
    total = None
    for side in range(SIDES):
        both = jnp.concatenate([sums[side], zero] if half == 0 else [zero, sums[side]], axis=1)
        if side != RY:
            both = pltpu.roll(both, (RY - side) % both.shape[1], 1)
        total = both if total is None else total + both
    return total


def beside_terms(source, n, column, x, flip):
    terms = []
    for m in range(n + 1):
        c = mirrored(m, x, flip)
        terms.append((source, c, c - column + 2 * RX * (1 - flip)))
    return terms


def early_kernel(angles, x, flip_ref, weights, own_a, near_a, own_b, near_b, totals):
    flip = flip_ref[0]

    def level(j, carry):
        for n in range(x):
            column = mirrored(n, x, flip)
            row = j * x + column
            for piece in range(angles // PART):
                at = pl.multiple_of(j * angles + piece * PART, PART)
                part = slice(piece * PART, (piece + 1) * PART)
                total = None
                for half, (own, near) in enumerate(((own_a, near_a), (own_b, near_b))):
                    terms = [(own, c, c - column + RX) for c in range(x)]
                    terms += beside_terms(near, n, column, x, flip)
                    term = spread(half_sums(weights, half, row, at, terms), half)
                    total = term if total is None else total + term
                totals[row, part, :] = total
        return carry

    lax.fori_loop(0, totals.shape[0] // x, level, 0)


def scalar_spec():
    return pl.BlockSpec(memory_space=pltpu.SMEM)


def early(flip, weights, own_a, near_a, own_b, near_b, angles, z, x, y):
    return pl.pallas_call(
        functools.partial(early_kernel, angles, x),
        out_shape=struct((z * x, angles, y), F32),
        in_specs=[scalar_spec()] + [spec()] * 5,
        out_specs=spec(),
        compiler_params=params(14),
        cost_estimate=cost(2 * weights.shape[1] * angles * z * x * y, 8 << 20),
        name="early",
    )(flip, weights, own_a, near_a, own_b, near_b)


def add_far_kernel(angles, x, flip_ref, weights, far, given, totals):
    flip = flip_ref[0]

    def level(j, carry):
        for n in range(x):
            column = mirrored(n, x, flip)
            row = j * x + column
            terms = beside_terms(far, n, column, x, flip)
            for piece in range(angles // PART):
                at = pl.multiple_of(j * angles + piece * PART, PART)
                part = slice(piece * PART, (piece + 1) * PART)
                sums = half_sums(weights, 0, row, at, terms)
                totals[row, part, :] = given[row, part, :] + spread(sums, 0)
        return carry

    lax.fori_loop(0, totals.shape[0] // x, level, 0)


def add_far(flip, weights, far, totals, angles, z, x, y):
    return pl.pallas_call(
        functools.partial(add_far_kernel, angles, x),
        out_shape=struct((z * x, angles, y), F32),
        in_specs=[scalar_spec()] + [spec()] * 3,
        out_specs=spec(),
        input_output_aliases={3: 0},
        compiler_params=params(14),
        cost_estimate=cost(weights.shape[1] * angles * z * x * y // 4, 8 << 20),
        name="add_far",
    )(flip, weights, far, totals)


def finish_kernel(angles, x, first, flip_ref, weights, totals, far, *rest):
    out, scratch = rest[-2:]
    flip = flip_ref[0]
    unswap = unswap_matrix(angles, x)
    base = pl.program_id(0) * ZB

    def level(j, carry):
        for n in range(x):
            column = mirrored(n, x, flip)
            row = (first + base + j) * x + column
            terms = beside_terms(far, n, column, x, flip)
            for piece in range(angles // PART):
                at = pl.multiple_of((base + j) * angles + piece * PART, PART)
                part = slice(piece * PART, (piece + 1) * PART)
                sums = half_sums(weights, 1, row, at, terms)
                total = totals[row, part, :] + spread(sums, 1)
                to = pl.multiple_of(column * angles + piece * PART, PART)
                scratch[pl.ds(to, PART), :] = total.astype(BF)
        moved = jnp.dot(unswap, scratch[...], preferred_element_type=F32)
        out[:, j] = moved.astype(BF).reshape(angles, x, out.shape[3])
        return carry

    lax.fori_loop(0, ZB, level, 0)


def finish(flip, weights, totals, far, done, first, shape):
    angles, _, x, y = shape
    planes = far.shape[1] // angles
    in_specs = [scalar_spec()] + [spec()] * 3
    operands = [flip, weights, totals, far]
    aliases = {}
    if done is not None:
        in_specs.append(pl.BlockSpec(memory_space=pl.ANY))
        operands.append(done)
        aliases = {4: 0}
    return pl.pallas_call(
        functools.partial(finish_kernel, angles, x, first),
        grid=(planes // ZB,),
        out_shape=struct(shape),
        in_specs=in_specs,
        out_specs=pl.BlockSpec((angles, ZB, x, y), lambda i: (0, first // ZB + i, 0, 0)),
        scratch_shapes=[pltpu.VMEM((angles * x, y), BF)],
        input_output_aliases=aliases,
        compiler_params=params(14),
        cost_estimate=cost(weights.shape[1] * angles * planes * x * y // 4, 3 << 20),
        name="finish",
    )(*operands)


def slant_matrix_of(slant_taper, band_offsets, offset_count):
    offset_index = jnp.arange(offset_count, dtype=jnp.int32)
    depth_shift = jnp.floor_divide(band_offsets[:, None] * offset_index[None, :], offset_count)
    reach_index = jnp.arange(slant_taper.shape[2], dtype=jnp.int32) - R
    inside_band = jnp.abs(reach_index[None, None, :] - depth_shift[:, :, None]) <= BAND
    return jnp.where(inside_band, slant_taper, jnp.zeros_like(slant_taper))


def exchange(x_up, x_down, axis):
    count = lax.axis_size(axis)
    up = [(i, i + 1) for i in range(count - 1)]
    down = [(j, i) for i, j in up]
    from_up = lax.ppermute(x_up, axis, up)
    from_down = lax.ppermute(x_down, axis, down)
    return from_up, from_down


def near_of(x, axis):
    count = lax.axis_size(axis)
    return lax.ppermute(x, axis, [(i, i ^ 1) for i in range(count)])


def far_of(x, axis):
    pairs = [(i, i + 1) for i in range(1, lax.axis_size(axis) - 1, 2)]
    return lax.ppermute(x, axis, pairs + [(j, i) for i, j in pairs])


def local(offset_image, dip_class, slant_taper, band_offsets, coefficients):
    h, z, x, y = offset_image.shape
    angles = slant_taper.shape[0]
    before, after = reach_tables(h, R)
    up_a, down_a = exchange(*pack(offset_image, before, after), "depth")
    slant = jnp.transpose(slant_matrix_of(slant_taper, band_offsets, h), (2, 0, 1))
    prepared = prepare(offset_image, coefficients, dip_class, slant, before, after)
    up_b, down_b, mid_a, mid_b, matrix, weights = prepared
    up_b, down_b = exchange(up_b, down_b, "depth")
    part_a, part_b = own_part(matrix, mid_a, mid_b, z)
    (own_a,) = gather(matrix, up_a, down_a, part_a, before, after, (z,))
    far_a = far_of(own_a, "gx")
    near_a = near_of(own_a, "gx")
    own_b, *parts = gather(matrix, up_b, down_b, part_b, before, after, LAST_PARTS)
    fars = []
    for part in parts:
        fars.append(far_of(part, "gx"))
    near_b = near_of(own_b, "gx")
    odd = (lax.axis_index("gx") % 2).astype(jnp.int32).reshape(1)
    totals = early(odd, weights, own_a, near_a, own_b, near_b, angles, z, x, y)
    totals = add_far(1 - odd, weights, far_a, totals, angles, z, x, y)
    done, first = None, 0
    for far, planes in zip(fars, LAST_PARTS):
        done = finish(1 - odd, weights, totals, far, done, first, (angles, z, x, y))
        first += planes
    return done


def solution(mesh):
    return jax.shard_map(
        local,
        mesh=mesh,
        in_specs=(P(None, "depth", "gx", None), P("depth", "gx", None), P(), P(), P()),
        out_specs=P(None, "depth", "gx", None),
        check_vma=False,
    )
```

```python
import functools

import jax
import jax.numpy as jnp
from jax import lax
from jax.experimental import pallas as pl
from jax.experimental.pallas import tpu as pltpu
from jax.sharding import PartitionSpec as P


R = 16
BAND = 2
RX = 4
RY = 1
REACH = R - BAND
ZB = 4
HALVES = 2
LAST_PARTS = (8, 8)
PART = 32
SIDES = 2 * RY + 1
BF = jnp.bfloat16
F32 = jnp.float32


def reach_tables(offsets, steps):
    before, after = [], []
    for k in range(1, steps + 1):
        low = [h for h in range(offsets) if -((-REACH * h) // offsets) + BAND >= k]
        high = [h for h in range(offsets) if (REACH * h) // offsets + BAND >= k]
        if low:
            before.append(low[0])
        if high:
            after.append(high[0])
    return before, after


def segments(firsts, offsets):
    out, at = [], 0
    for first in firsts:
        out.append((at, offsets - first))
        at += offsets - first
    return out, at


def spec():
    return pl.BlockSpec(memory_space=pltpu.VMEM)


def params(mib):
    return pltpu.CompilerParams(vmem_limit_bytes=mib << 20)


def cost(flops, moved):
    return pl.CostEstimate(flops=flops, bytes_accessed=moved, transcendentals=0)


def struct(shape, kind=BF):
    return jax.ShapeDtypeStruct(shape, kind)


def swap_matrix(offsets, columns):
    n = offsets * columns
    row = lax.broadcasted_iota(jnp.int32, (n, n), 0)
    col = lax.broadcasted_iota(jnp.int32, (n, n), 1)
    hit = col == (row % offsets) * columns + row // offsets
    return jnp.where(hit, 1.0, 0.0).astype(BF)


def unswap_matrix(angles, columns):
    n = angles * columns
    row = lax.broadcasted_iota(jnp.int32, (n, n), 0)
    col = lax.broadcasted_iota(jnp.int32, (n, n), 1)
    hit = row == (col % angles) * columns + col // angles
    return jnp.where(hit, 1.0, 0.0).astype(BF)


def pack_half(before, after, half, image, up, down):
    h, z = image.shape[:2]
    width = up.shape[2]
    lanes = slice(half * width, (half + 1) * width)
    for k, (at, n) in enumerate(segments(before, h)[0]):
        up[at : at + n] = image[h - n : h, z - 1 - k, :, lanes]
    for k, (at, n) in enumerate(segments(after, h)[0]):
        down[at : at + n] = image[h - n : h, k, :, lanes]


def pack_shapes(image, before, after):
    h, _, x, y = image.shape
    n_up, n_down = segments(before, h)[1], segments(after, h)[1]
    return struct((n_up, x, y // HALVES)), struct((n_down, x, y // HALVES))


def pack_kernel(before, after, image, up, down, part, sem):
    copy = pltpu.make_async_copy(image.at[:, :, :, pl.ds(0, part.shape[3])], part, sem)
    copy.start()
    copy.wait()
    pack_half(before, after, 0, part, up, down)


def pack(image, before, after):
    h, z, x, y = image.shape
    return pl.pallas_call(
        functools.partial(pack_kernel, before, after),
        out_shape=pack_shapes(image, before, after),
        in_specs=[pl.BlockSpec(memory_space=pltpu.HBM)],
        out_specs=(spec(),) * 2,
        scratch_shapes=[pltpu.VMEM((h, z, x, y // HALVES), BF), pltpu.SemaphoreType.DMA],
        compiler_params=params(62),
        name="pack",
    )(image)


def prepare_kernel(before, after, image, coefficients, dip, slant, up, down, *outs):
    columns, (matrix, weights) = outs[:HALVES], outs[HALVES:]
    h, z, x, y = image.shape
    width = y // HALVES
    pack_half(before, after, 1, image, up, down)
    swap = swap_matrix(h, x)
    for level in range(z):
        plane = image[:, level].reshape(h * x, y)
        moved = jnp.dot(swap, plane, preferred_element_type=F32).astype(BF)
        for half in range(HALVES):
            for c in range(x):
                at = (c % 2) * width
                columns[half][c // 2, level * h : (level + 1) * h, at : at + width] = moved[
                    c * h : (c + 1) * h, half * width : (half + 1) * width
                ]
    steps, angles, _ = slant.shape
    zero = jnp.zeros((angles, h), BF)
    for j in range(ZB):
        for t in range((steps + ZB - 1) // 2):
            pair = [slant[d] if 0 <= d < steps else zero for d in (2 * t - j, 2 * t + 1 - j)]
            matrix[j * angles : (j + 1) * angles, 2 * t * h : 2 * (t + 1) * h] = jnp.concatenate(
                pair, axis=1
            )
    lane = lax.broadcasted_iota(jnp.int32, (z * x, y), 1)
    classes = dip[...]
    tests = [classes == q for q in range(1, coefficients.shape[0])]
    for t in range(weights.shape[1]):
        w = jnp.full((z * x, y), coefficients[0, t], F32)
        for q, test in enumerate(tests):
            w = jnp.where(test, coefficients[q + 1, t], w)
        shift = t % SIDES - RY
        if shift:
            w = pltpu.roll(w, shift % y, 1)
            w = jnp.where(lane < shift if shift > 0 else lane >= y + shift, 0.0, w)
        for half in range(HALVES):
            weights[half, t] = w[:, half * width : (half + 1) * width]


def prepare(image, coefficients, dip, slant, before, after):
    h, z, x, y = image.shape
    steps, angles, _ = slant.shape
    taps = coefficients.shape[1]
    return pl.pallas_call(
        functools.partial(prepare_kernel, before, after),
        out_shape=(
            *pack_shapes(image, before, after),
            *(struct((x // 2, z * h, 2 * y // HALVES)) for _ in range(HALVES)),
            struct((ZB * angles, (steps + ZB - 1) * h)),
            struct((HALVES, taps, z * x, y // HALVES), F32),
        ),
        in_specs=[spec(), pl.BlockSpec(memory_space=pltpu.SMEM), spec(), spec()],
        out_specs=(spec(),) * (4 + HALVES),
        compiler_params=params(14),
        cost_estimate=cost(2 * h * x * h * x * y * z, 8 << 20),
        name="prepare",
    )(image, coefficients, dip.reshape(z * x, y), slant)


def unpack(swap, source, pieces, starts, target):
    h, x = swap.shape[0] // source.shape[1], source.shape[1]
    width = source.shape[2]
    for k in range(0, len(pieces), 2):
        pair = [pieces[min(i, len(pieces) - 1)] for i in (k, k + 1)]
        planes = [source[at + n - h : at + n].reshape(h * x, width) for at, n in pair]
        moved = jnp.dot(swap, jnp.concatenate(planes, axis=1), preferred_element_type=F32)
        moved = moved.astype(BF)
        for i in range(min(2, len(pieces) - k)):
            rows = slice(starts[k + i] * h, (starts[k + i] + 1) * h)
            for c in range(x):
                at = (c % 2) * width
                target[c // 2, rows, at : at + width] = moved[
                    c * h : (c + 1) * h, i * width : (i + 1) * width
                ]


def partial_kernel(matrix, mid_a, mid_b, out_a, out_b):
    h = matrix.shape[1] // (2 * R + ZB)
    for mid, out in ((mid_a, out_a), (mid_b, out_b)):
        n_mid = mid.shape[1]
        for zb in range(out.shape[0]):
            n_low = n_mid - zb * ZB * h
            for c in range(mid.shape[0]):
                out[zb, c] = jnp.dot(
                    matrix[:, n_low : n_low + n_mid], mid[c], preferred_element_type=F32
                )


def own_part(matrix, mid_a, mid_b, z):
    pairs, rows, width = mid_a.shape
    m = matrix.shape[0]
    return pl.pallas_call(
        partial_kernel,
        out_shape=(struct((z // ZB, pairs, m, width), F32),) * 2,
        in_specs=[spec()] * 3,
        out_specs=(spec(),) * 2,
        compiler_params=params(14),
        cost_estimate=cost(4 * (z // ZB) * m * rows * pairs * width, 9 << 20),
        name="own_part",
    )(matrix, mid_a, mid_b)


def gather_kernel(before, after, parts, matrix, up, down, given, *rest):
    (own, *outs), (low, high) = rest[:-2], rest[-2:]
    x = up.shape[1]
    m = matrix.shape[0]
    h = matrix.shape[1] // (2 * R + ZB)
    tile = ZB * h
    swap = swap_matrix(h, x)
    unpack(swap, up, segments(before, h)[0], [R - 1 - k for k in range(R)], low)
    unpack(swap, down, segments(after, h)[0], list(range(R)), high)
    for k in range(len(after), R):
        high[:, k * h : (k + 1) * h, :] = jnp.zeros((x // 2, h, high.shape[2]), BF)
    zb = 0
    n_mid = matrix.shape[1] - ZB * h - low.shape[1]
    for index, planes in enumerate(parts):
        for block in range(planes // ZB):
            n_low = low.shape[1] - zb * tile
            n_high = (zb + 1) * tile
            for c in range(x // 2):
                total = given[zb, c] + jnp.dot(
                    matrix[:, :n_low], low[c, zb * tile :, :], preferred_element_type=F32
                )
                total += jnp.dot(
                    matrix[:, n_low + n_mid :], high[c, :n_high, :], preferred_element_type=F32
                )
                moved = total.astype(BF)
                width = moved.shape[1] // 2
                for side in range(2):
                    piece = moved[:, side * width : (side + 1) * width]
                    own[2 * c + side, zb * m : (zb + 1) * m, :] = piece
                    if outs:
                        outs[index][2 * c + side, block * m : (block + 1) * m, :] = piece
            zb += 1


def gather(matrix, up, down, given, before, after, parts):
    _, pairs, _, width = given.shape
    rows = sum(parts) * (matrix.shape[1] // (2 * R + ZB))
    per_plane = matrix.shape[0] // ZB
    sizes = (sum(parts), *(parts if len(parts) > 1 else ()))
    return pl.pallas_call(
        functools.partial(gather_kernel, before, after, parts),
        out_shape=tuple(struct((2 * pairs, n * per_plane, width // 2)) for n in sizes),
        in_specs=[spec()] * 4,
        out_specs=(spec(),) * len(sizes),
        scratch_shapes=[pltpu.VMEM((pairs, rows, width), BF)] * 2,
        compiler_params=params(14),
        cost_estimate=cost(2 * sum(parts) * per_plane * matrix.shape[1] * pairs * width, 6 << 20),
        name="gather",
    )(matrix, up, down, given)


def mirrored(n, count, flip):
    return n + flip * (count - 1 - 2 * n)


def half_sums(weights, half, row, at, terms):
    sums = [None] * SIDES
    for source, c, step in terms:
        values = source[c, pl.ds(at, PART), :].astype(F32)
        for side in range(SIDES):
            w = weights[half, step * SIDES + side, pl.ds(row, 1), :]
            term = w * values
            sums[side] = term if sums[side] is None else sums[side] + term
    return sums


def spread(sums, half):
    width = sums[0].shape[1]
    lane = lax.broadcasted_iota(jnp.int32, sums[0].shape, 1)
    here, there = sums[RY], jnp.zeros_like(sums[0])
    for side in range(SIDES):
        shift = RY - side
        if shift == 0:
            continue
        moved = pltpu.roll(sums[side], shift % width, 1)
        if (shift > 0) == (half == 0):
            edge = lane < shift if shift > 0 else lane >= width + shift
            here = here + jnp.where(edge, 0.0, moved)
            there = there + jnp.where(edge, moved, 0.0)
        else:
            here = here + moved
    return jnp.concatenate([here, there] if half == 0 else [there, here], axis=1)


def beside_terms(source, n, column, x, flip):
    terms = []
    for m in range(n + 1):
        c = mirrored(m, x, flip)
        terms.append((source, c, c - column + 2 * RX * (1 - flip)))
    return terms


def early_kernel(half, angles, x, flip_ref, weights, own, near, *rest):
    totals = rest[-1]
    flip = flip_ref[0]

    def level(j, carry):
        for n in range(x):
            column = mirrored(n, x, flip)
            row = j * x + column
            terms = [(own, c, c - column + RX) for c in range(x)]
            terms += beside_terms(near, n, column, x, flip)
            for piece in range(angles // PART):
                at = pl.multiple_of(j * angles + piece * PART, PART)
                part = slice(piece * PART, (piece + 1) * PART)
                total = spread(half_sums(weights, half, row, at, terms), half)
                if len(rest) > 1:
                    total = total + rest[0][row, part, :]
                totals[row, part, :] = total
        return carry

    lax.fori_loop(0, totals.shape[0] // x, level, 0)


def scalar_spec():
    return pl.BlockSpec(memory_space=pltpu.SMEM)


def early(flip, weights, own, near, totals, half, angles, z, x, y):
    operands = [flip, weights, own, near] + ([] if totals is None else [totals])
    return pl.pallas_call(
        functools.partial(early_kernel, half, angles, x),
        out_shape=struct((z * x, angles, y), F32),
        in_specs=[scalar_spec()] + [spec()] * (len(operands) - 1),
        out_specs=spec(),
        compiler_params=params(14),
        cost_estimate=cost(weights.shape[1] * angles * z * x * y, 10 << 20),
        name="early",
    )(*operands)


def add_far_kernel(angles, x, flip_ref, weights, far, given, totals):
    flip = flip_ref[0]

    def level(j, carry):
        for n in range(x):
            column = mirrored(n, x, flip)
            row = j * x + column
            terms = beside_terms(far, n, column, x, flip)
            for piece in range(angles // PART):
                at = pl.multiple_of(j * angles + piece * PART, PART)
                part = slice(piece * PART, (piece + 1) * PART)
                sums = half_sums(weights, 0, row, at, terms)
                totals[row, part, :] = given[row, part, :] + spread(sums, 0)
        return carry

    lax.fori_loop(0, totals.shape[0] // x, level, 0)


def add_far(flip, weights, far, totals, angles, z, x, y):
    return pl.pallas_call(
        functools.partial(add_far_kernel, angles, x),
        out_shape=struct((z * x, angles, y), F32),
        in_specs=[scalar_spec()] + [spec()] * 3,
        out_specs=spec(),
        compiler_params=params(14),
        cost_estimate=cost(weights.shape[1] * angles * z * x * y // 4, 8 << 20),
        name="add_far",
    )(flip, weights, far, totals)


def finish_kernel(angles, x, first, flip_ref, weights, totals, far, *rest):
    out, scratch, unswap = rest[-3:]
    flip = flip_ref[0]
    base = pl.program_id(0) * ZB

    @pl.when(pl.program_id(0) == 0)
    def _():
        unswap[...] = unswap_matrix(angles, x)

    def level(j, carry):
        for n in range(x):
            column = mirrored(n, x, flip)
            row = (first + base + j) * x + column
            terms = beside_terms(far, n, column, x, flip)
            for piece in range(angles // PART):
                at = pl.multiple_of(j * angles + piece * PART, PART)
                part = slice(piece * PART, (piece + 1) * PART)
                sums = half_sums(weights, 1, row, at, terms)
                total = totals[row, part, :] + spread(sums, 1)
                to = pl.multiple_of(column * angles + piece * PART, PART)
                scratch[pl.ds(to, PART), :] = total.astype(BF)
        moved = jnp.dot(unswap[...], scratch[...], preferred_element_type=F32)
        out[:, j] = moved.astype(BF).reshape(angles, x, out.shape[3])
        return carry

    lax.fori_loop(0, ZB, level, 0)


def finish(flip, weights, totals, far, done, first, shape):
    angles, _, x, y = shape
    planes = far.shape[1] // angles
    far_spec = pl.BlockSpec((x, ZB * angles, far.shape[2]), lambda i: (0, i, 0))
    in_specs = [scalar_spec(), spec(), spec(), far_spec]
    operands = [flip, weights, totals, far]
    aliases = {}
    if done is not None:
        in_specs.append(pl.BlockSpec(memory_space=pl.ANY))
        operands.append(done)
        aliases = {4: 0}
    return pl.pallas_call(
        functools.partial(finish_kernel, angles, x, first),
        grid=(planes // ZB,),
        out_shape=struct(shape),
        in_specs=in_specs,
        out_specs=pl.BlockSpec((angles, ZB, x, y), lambda i: (0, first // ZB + i, 0, 0)),
        scratch_shapes=[pltpu.VMEM((angles * x, y), BF), pltpu.VMEM((angles * x,) * 2, BF)],
        input_output_aliases=aliases,
        compiler_params=params(14),
        cost_estimate=cost(weights.shape[1] * angles * planes * x * y // 4, 3 << 20),
        name="finish",
    )(*operands)


def slant_matrix_of(slant_taper, band_offsets, offset_count):
    offset_index = jnp.arange(offset_count, dtype=jnp.int32)
    depth_shift = jnp.floor_divide(band_offsets[:, None] * offset_index[None, :], offset_count)
    reach_index = jnp.arange(slant_taper.shape[2], dtype=jnp.int32) - R
    inside_band = jnp.abs(reach_index[None, None, :] - depth_shift[:, :, None]) <= BAND
    return jnp.where(inside_band, slant_taper, jnp.zeros_like(slant_taper))


def exchange(x_up, x_down, axis):
    count = lax.axis_size(axis)
    up = [(i, i + 1) for i in range(count - 1)]
    down = [(j, i) for i, j in up]
    from_up = lax.ppermute(x_up, axis, up)
    from_down = lax.ppermute(x_down, axis, down)
    return from_up, from_down


def near_of(x, axis):
    count = lax.axis_size(axis)
    return lax.ppermute(x, axis, [(i, i ^ 1) for i in range(count)])


def far_of(x, axis):
    pairs = [(i, i + 1) for i in range(1, lax.axis_size(axis) - 1, 2)]
    return lax.ppermute(x, axis, pairs + [(j, i) for i, j in pairs])


def local(offset_image, dip_class, slant_taper, band_offsets, coefficients):
    h, z, x, y = offset_image.shape
    angles = slant_taper.shape[0]
    before, after = reach_tables(h, R)
    up_a, down_a = exchange(*pack(offset_image, before, after), "depth")
    slant = jnp.transpose(slant_matrix_of(slant_taper, band_offsets, h), (2, 0, 1))
    prepared = prepare(offset_image, coefficients, dip_class, slant, before, after)
    up_b, down_b, mid_a, mid_b, matrix, weights = prepared
    up_b, down_b = exchange(up_b, down_b, "depth")
    part_a, part_b = own_part(matrix, mid_a, mid_b, z)
    (own_a,) = gather(matrix, up_a, down_a, part_a, before, after, (z,))
    far_a = far_of(own_a, "gx")
    near_a = near_of(own_a, "gx")
    own_b, *parts = gather(matrix, up_b, down_b, part_b, before, after, LAST_PARTS)
    fars = []
    for part in parts:
        fars.append(far_of(part, "gx"))
    near_b = near_of(own_b, "gx")
    odd = (lax.axis_index("gx") % 2).astype(jnp.int32).reshape(1)
    totals = early(odd, weights, own_a, near_a, None, 0, angles, z, x, y)
    totals = early(odd, weights, own_b, near_b, totals, 1, angles, z, x, y)
    totals = add_far(1 - odd, weights, far_a, totals, angles, z, x, y)
    done, first = None, 0
    for far, planes in zip(fars, LAST_PARTS):
        done = finish(1 - odd, weights, totals, far, done, first, (angles, z, x, y))
        first += planes
    return done


def solution(mesh):
    return jax.shard_map(
        local,
        mesh=mesh,
        in_specs=(P(None, "depth", "gx", None), P("depth", "gx", None), P(), P(), P()),
        out_specs=P(None, "depth", "gx", None),
        check_vma=False,
    )
```

```python
import functools

import jax
import jax.numpy as jnp
from jax import lax
from jax.experimental import pallas as pl
from jax.experimental.pallas import tpu as pltpu
from jax.sharding import PartitionSpec as P


R = 16
BAND = 2
RX = 4
RY = 1
REACH = R - BAND
ZB = 4
HALVES = 2
LAST_PARTS = (8, 4, 4)
PART = 32
SIDES = 2 * RY + 1
BF = jnp.bfloat16
F32 = jnp.float32


def reach_tables(offsets, steps):
    before, after = [], []
    for k in range(1, steps + 1):
        low = [h for h in range(offsets) if -((-REACH * h) // offsets) + BAND >= k]
        high = [h for h in range(offsets) if (REACH * h) // offsets + BAND >= k]
        if low:
            before.append(low[0])
        if high:
            after.append(high[0])
    return before, after


def segments(firsts, offsets):
    out, at = [], 0
    for first in firsts:
        out.append((at, offsets - first))
        at += offsets - first
    return out, at


def spec():
    return pl.BlockSpec(memory_space=pltpu.VMEM)


def params(mib):
    return pltpu.CompilerParams(vmem_limit_bytes=mib << 20)


def cost(flops, moved):
    return pl.CostEstimate(flops=flops, bytes_accessed=moved, transcendentals=0)


def struct(shape, kind=BF):
    return jax.ShapeDtypeStruct(shape, kind)


def swap_matrix(offsets, columns):
    n = offsets * columns
    row = lax.broadcasted_iota(jnp.int32, (n, n), 0)
    col = lax.broadcasted_iota(jnp.int32, (n, n), 1)
    hit = col == (row % offsets) * columns + row // offsets
    return jnp.where(hit, 1.0, 0.0).astype(BF)


def unswap_matrix(angles, columns):
    n = angles * columns
    row = lax.broadcasted_iota(jnp.int32, (n, n), 0)
    col = lax.broadcasted_iota(jnp.int32, (n, n), 1)
    hit = row == (col % angles) * columns + col // angles
    return jnp.where(hit, 1.0, 0.0).astype(BF)


def pack_half(before, after, half, image, up, down):
    h, z = image.shape[:2]
    width = up.shape[2]
    lanes = slice(half * width, (half + 1) * width)
    for k, (at, n) in enumerate(segments(before, h)[0]):
        up[at : at + n] = image[h - n : h, z - 1 - k, :, lanes]
    for k, (at, n) in enumerate(segments(after, h)[0]):
        down[at : at + n] = image[h - n : h, k, :, lanes]


def pack_shapes(image, before, after):
    h, _, x, y = image.shape
    n_up, n_down = segments(before, h)[1], segments(after, h)[1]
    return struct((n_up, x, y // HALVES)), struct((n_down, x, y // HALVES))


def pack_kernel(before, after, image, up, down, part, sem):
    copy = pltpu.make_async_copy(image.at[:, :, :, pl.ds(0, part.shape[3])], part, sem)
    copy.start()
    copy.wait()
    pack_half(before, after, 0, part, up, down)


def pack(image, before, after):
    h, z, x, y = image.shape
    return pl.pallas_call(
        functools.partial(pack_kernel, before, after),
        out_shape=pack_shapes(image, before, after),
        in_specs=[pl.BlockSpec(memory_space=pltpu.HBM)],
        out_specs=(spec(),) * 2,
        scratch_shapes=[pltpu.VMEM((h, z, x, y // HALVES), BF), pltpu.SemaphoreType.DMA],
        compiler_params=params(62),
        name="pack",
    )(image)


def prepare_kernel(before, after, image, coefficients, dip, slant, up, down, *outs):
    columns, (matrix, weights) = outs[:HALVES], outs[HALVES:]
    h, z, x, y = image.shape
    width = y // HALVES
    pack_half(before, after, 1, image, up, down)
    swap = swap_matrix(h, x)
    for level in range(z):
        plane = image[:, level].reshape(h * x, y)
        moved = jnp.dot(swap, plane, preferred_element_type=F32).astype(BF)
        for half in range(HALVES):
            for c in range(x):
                at = (c % 2) * width
                columns[half][c // 2, level * h : (level + 1) * h, at : at + width] = moved[
                    c * h : (c + 1) * h, half * width : (half + 1) * width
                ]
    steps, angles, _ = slant.shape
    zero = jnp.zeros((angles, h), BF)
    for j in range(ZB):
        for t in range((steps + ZB - 1) // 2):
            pair = [slant[d] if 0 <= d < steps else zero for d in (2 * t - j, 2 * t + 1 - j)]
            matrix[j * angles : (j + 1) * angles, 2 * t * h : 2 * (t + 1) * h] = jnp.concatenate(
                pair, axis=1
            )
    lane = lax.broadcasted_iota(jnp.int32, (z * x, y), 1)
    classes = dip[...]
    tests = [classes == q for q in range(1, coefficients.shape[0])]
    for t in range(weights.shape[1]):
        w = jnp.full((z * x, y), coefficients[0, t], F32)
        for q, test in enumerate(tests):
            w = jnp.where(test, coefficients[q + 1, t], w)
        shift = t % SIDES - RY
        if shift:
            w = pltpu.roll(w, shift % y, 1)
            w = jnp.where(lane < shift if shift > 0 else lane >= y + shift, 0.0, w)
        for half in range(HALVES):
            weights[half, t] = w[:, half * width : (half + 1) * width]


def prepare(image, coefficients, dip, slant, before, after):
    h, z, x, y = image.shape
    steps, angles, _ = slant.shape
    taps = coefficients.shape[1]
    return pl.pallas_call(
        functools.partial(prepare_kernel, before, after),
        out_shape=(
            *pack_shapes(image, before, after),
            *(struct((x // 2, z * h, 2 * y // HALVES)) for _ in range(HALVES)),
            struct((ZB * angles, (steps + ZB - 1) * h)),
            struct((HALVES, taps, z * x, y // HALVES), F32),
        ),
        in_specs=[spec(), pl.BlockSpec(memory_space=pltpu.SMEM), spec(), spec()],
        out_specs=(spec(),) * (4 + HALVES),
        compiler_params=params(14),
        cost_estimate=cost(2 * h * x * h * x * y * z, 8 << 20),
        name="prepare",
    )(image, coefficients, dip.reshape(z * x, y), slant)


def unpack(swap, source, pieces, starts, target):
    h, x = swap.shape[0] // source.shape[1], source.shape[1]
    width = source.shape[2]
    for k in range(0, len(pieces), 2):
        pair = [pieces[min(i, len(pieces) - 1)] for i in (k, k + 1)]
        planes = [source[at + n - h : at + n].reshape(h * x, width) for at, n in pair]
        moved = jnp.dot(swap, jnp.concatenate(planes, axis=1), preferred_element_type=F32)
        moved = moved.astype(BF)
        for i in range(min(2, len(pieces) - k)):
            rows = slice(starts[k + i] * h, (starts[k + i] + 1) * h)
            for c in range(x):
                at = (c % 2) * width
                target[c // 2, rows, at : at + width] = moved[
                    c * h : (c + 1) * h, i * width : (i + 1) * width
                ]


def partial_kernel(matrix, mid_a, mid_b, out_a, out_b):
    h = matrix.shape[1] // (2 * R + ZB)
    for mid, out in ((mid_a, out_a), (mid_b, out_b)):
        n_mid = mid.shape[1]
        for zb in range(out.shape[0]):
            n_low = n_mid - zb * ZB * h
            for c in range(mid.shape[0]):
                out[zb, c] = jnp.dot(
                    matrix[:, n_low : n_low + n_mid], mid[c], preferred_element_type=F32
                )


def own_part(matrix, mid_a, mid_b, z):
    pairs, rows, width = mid_a.shape
    m = matrix.shape[0]
    return pl.pallas_call(
        partial_kernel,
        out_shape=(struct((z // ZB, pairs, m, width), F32),) * 2,
        in_specs=[spec()] * 3,
        out_specs=(spec(),) * 2,
        compiler_params=params(14),
        cost_estimate=cost(4 * (z // ZB) * m * rows * pairs * width, 9 << 20),
        name="own_part",
    )(matrix, mid_a, mid_b)


def gather_kernel(before, after, parts, matrix, up, down, given, *rest):
    (own, *outs), (low, high) = rest[:-2], rest[-2:]
    x = up.shape[1]
    m = matrix.shape[0]
    h = matrix.shape[1] // (2 * R + ZB)
    tile = ZB * h
    swap = swap_matrix(h, x)
    unpack(swap, up, segments(before, h)[0], [R - 1 - k for k in range(R)], low)
    unpack(swap, down, segments(after, h)[0], list(range(R)), high)
    for k in range(len(after), R):
        high[:, k * h : (k + 1) * h, :] = jnp.zeros((x // 2, h, high.shape[2]), BF)
    zb = 0
    n_mid = matrix.shape[1] - ZB * h - low.shape[1]
    for index, planes in enumerate(parts):
        for block in range(planes // ZB):
            n_low = low.shape[1] - zb * tile
            n_high = (zb + 1) * tile
            for c in range(x // 2):
                total = given[zb, c] + jnp.dot(
                    matrix[:, :n_low], low[c, zb * tile :, :], preferred_element_type=F32
                )
                total += jnp.dot(
                    matrix[:, n_low + n_mid :], high[c, :n_high, :], preferred_element_type=F32
                )
                moved = total.astype(BF)
                width = moved.shape[1] // 2
                for side in range(2):
                    piece = moved[:, side * width : (side + 1) * width]
                    own[2 * c + side, zb * m : (zb + 1) * m, :] = piece
                    if outs:
                        outs[index][2 * c + side, block * m : (block + 1) * m, :] = piece
            zb += 1


def gather(matrix, up, down, given, before, after, parts):
    _, pairs, _, width = given.shape
    rows = sum(parts) * (matrix.shape[1] // (2 * R + ZB))
    per_plane = matrix.shape[0] // ZB
    sizes = (sum(parts), *(parts if len(parts) > 1 else ()))
    return pl.pallas_call(
        functools.partial(gather_kernel, before, after, parts),
        out_shape=tuple(struct((2 * pairs, n * per_plane, width // 2)) for n in sizes),
        in_specs=[spec()] * 4,
        out_specs=(spec(),) * len(sizes),
        scratch_shapes=[pltpu.VMEM((pairs, rows, width), BF)] * 2,
        compiler_params=params(14),
        cost_estimate=cost(2 * sum(parts) * per_plane * matrix.shape[1] * pairs * width, 6 << 20),
        name="gather",
    )(matrix, up, down, given)


def mirrored(n, count, flip):
    return n + flip * (count - 1 - 2 * n)


def half_sums(weights, half, row, at, terms):
    sums = [None] * SIDES
    for source, c, step in terms:
        values = source[c, pl.ds(at, PART), :].astype(F32)
        for side in range(SIDES):
            w = weights[half, step * SIDES + side, pl.ds(row, 1), :]
            term = w * values
            sums[side] = term if sums[side] is None else sums[side] + term
    return sums


def spread(sums, half):
    width = sums[0].shape[1]
    lane = lax.broadcasted_iota(jnp.int32, sums[0].shape, 1)
    here, there = sums[RY], jnp.zeros_like(sums[0])
    for side in range(SIDES):
        shift = RY - side
        if shift == 0:
            continue
        moved = pltpu.roll(sums[side], shift % width, 1)
        if (shift > 0) == (half == 0):
            edge = lane < shift if shift > 0 else lane >= width + shift
            here = here + jnp.where(edge, 0.0, moved)
            there = there + jnp.where(edge, moved, 0.0)
        else:
            here = here + moved
    return jnp.concatenate([here, there] if half == 0 else [there, here], axis=1)


def beside_terms(source, n, column, x, flip):
    terms = []
    for m in range(n + 1):
        c = mirrored(m, x, flip)
        terms.append((source, c, c - column + 2 * RX * (1 - flip)))
    return terms


def early_kernel(half, angles, x, flip_ref, weights, own, near, *rest):
    totals = rest[-1]
    flip = flip_ref[0]

    def level(j, carry):
        for n in range(x):
            column = mirrored(n, x, flip)
            row = j * x + column
            terms = [(own, c, c - column + RX) for c in range(x)]
            terms += beside_terms(near, n, column, x, flip)
            for piece in range(angles // PART):
                at = pl.multiple_of(j * angles + piece * PART, PART)
                part = slice(piece * PART, (piece + 1) * PART)
                total = spread(half_sums(weights, half, row, at, terms), half)
                if len(rest) > 1:
                    total = total + rest[0][row, part, :]
                totals[row, part, :] = total
        return carry

    lax.fori_loop(0, totals.shape[0] // x, level, 0)


def scalar_spec():
    return pl.BlockSpec(memory_space=pltpu.SMEM)


def early(flip, weights, own, near, totals, half, angles, z, x, y):
    operands = [flip, weights, own, near] + ([] if totals is None else [totals])
    return pl.pallas_call(
        functools.partial(early_kernel, half, angles, x),
        out_shape=struct((z * x, angles, y), F32),
        in_specs=[scalar_spec()] + [spec()] * (len(operands) - 1),
        out_specs=spec(),
        compiler_params=params(14),
        cost_estimate=cost(weights.shape[1] * angles * z * x * y, 10 << 20),
        name="early",
    )(*operands)


def add_far_kernel(angles, x, flip_ref, weights, far, given, totals):
    flip = flip_ref[0]

    def level(j, carry):
        for n in range(x):
            column = mirrored(n, x, flip)
            row = j * x + column
            terms = beside_terms(far, n, column, x, flip)
            for piece in range(angles // PART):
                at = pl.multiple_of(j * angles + piece * PART, PART)
                part = slice(piece * PART, (piece + 1) * PART)
                sums = half_sums(weights, 0, row, at, terms)
                totals[row, part, :] = given[row, part, :] + spread(sums, 0)
        return carry

    lax.fori_loop(0, totals.shape[0] // x, level, 0)


def add_far(flip, weights, far, totals, angles, z, x, y):
    return pl.pallas_call(
        functools.partial(add_far_kernel, angles, x),
        out_shape=struct((z * x, angles, y), F32),
        in_specs=[scalar_spec()] + [spec()] * 3,
        out_specs=spec(),
        compiler_params=params(14),
        cost_estimate=cost(weights.shape[1] * angles * z * x * y // 4, 8 << 20),
        name="add_far",
    )(flip, weights, far, totals)


def finish_kernel(angles, x, first, flip_ref, weights, totals, far, *rest):
    out, scratch, unswap = rest[-3:]
    flip = flip_ref[0]
    base = pl.program_id(0) * ZB

    @pl.when(pl.program_id(0) == 0)
    def _():
        unswap[...] = unswap_matrix(angles, x)

    for j in range(ZB):
        for n in range(x):
            column = mirrored(n, x, flip)
            row = (first + base + j) * x + column
            terms = beside_terms(far, n, column, x, flip)
            for piece in range(angles // PART):
                at = j * angles + piece * PART
                part = slice(piece * PART, (piece + 1) * PART)
                sums = half_sums(weights, 1, row, at, terms)
                total = totals[row, part, :] + spread(sums, 1)
                to = pl.multiple_of(column * angles + piece * PART, PART)
                scratch[j, pl.ds(to, PART), :] = total.astype(BF)
        moved = jnp.dot(unswap[...], scratch[j], preferred_element_type=F32)
        out[:, j] = moved.astype(BF).reshape(angles, x, out.shape[3])


def finish(flip, weights, totals, far, done, first, shape):
    angles, _, x, y = shape
    planes = far.shape[1] // angles
    far_spec = pl.BlockSpec((x, ZB * angles, far.shape[2]), lambda i: (0, i, 0))
    in_specs = [scalar_spec(), spec(), spec(), far_spec]
    operands = [flip, weights, totals, far]
    aliases = {}
    if done is not None:
        in_specs.append(pl.BlockSpec(memory_space=pl.ANY))
        operands.append(done)
        aliases = {4: 0}
    return pl.pallas_call(
        functools.partial(finish_kernel, angles, x, first),
        grid=(planes // ZB,),
        out_shape=struct(shape),
        in_specs=in_specs,
        out_specs=pl.BlockSpec((angles, ZB, x, y), lambda i: (0, first // ZB + i, 0, 0)),
        scratch_shapes=[pltpu.VMEM((ZB, angles * x, y), BF), pltpu.VMEM((angles * x,) * 2, BF)],
        input_output_aliases=aliases,
        compiler_params=params(14),
        cost_estimate=cost(weights.shape[1] * angles * planes * x * y // 4, 3 << 20),
        name="finish",
    )(*operands)


def slant_matrix_of(slant_taper, band_offsets, offset_count):
    offset_index = jnp.arange(offset_count, dtype=jnp.int32)
    depth_shift = jnp.floor_divide(band_offsets[:, None] * offset_index[None, :], offset_count)
    reach_index = jnp.arange(slant_taper.shape[2], dtype=jnp.int32) - R
    inside_band = jnp.abs(reach_index[None, None, :] - depth_shift[:, :, None]) <= BAND
    return jnp.where(inside_band, slant_taper, jnp.zeros_like(slant_taper))


def exchange(x_up, x_down, axis):
    count = lax.axis_size(axis)
    up = [(i, i + 1) for i in range(count - 1)]
    down = [(j, i) for i, j in up]
    from_up = lax.ppermute(x_up, axis, up)
    from_down = lax.ppermute(x_down, axis, down)
    return from_up, from_down


def near_of(x, axis):
    count = lax.axis_size(axis)
    return lax.ppermute(x, axis, [(i, i ^ 1) for i in range(count)])


def far_of(x, axis):
    pairs = [(i, i + 1) for i in range(1, lax.axis_size(axis) - 1, 2)]
    return lax.ppermute(x, axis, pairs + [(j, i) for i, j in pairs])


def local(offset_image, dip_class, slant_taper, band_offsets, coefficients):
    h, z, x, y = offset_image.shape
    angles = slant_taper.shape[0]
    before, after = reach_tables(h, R)
    up_a, down_a = exchange(*pack(offset_image, before, after), "depth")
    slant = jnp.transpose(slant_matrix_of(slant_taper, band_offsets, h), (2, 0, 1))
    prepared = prepare(offset_image, coefficients, dip_class, slant, before, after)
    up_b, down_b, mid_a, mid_b, matrix, weights = prepared
    up_b, down_b = exchange(up_b, down_b, "depth")
    part_a, part_b = own_part(matrix, mid_a, mid_b, z)
    (own_a,) = gather(matrix, up_a, down_a, part_a, before, after, (z,))
    far_a = far_of(own_a, "gx")
    near_a = near_of(own_a, "gx")
    own_b, *parts = gather(matrix, up_b, down_b, part_b, before, after, LAST_PARTS)
    fars = []
    for part in parts:
        fars.append(far_of(part, "gx"))
    near_b = near_of(own_b, "gx")
    odd = (lax.axis_index("gx") % 2).astype(jnp.int32).reshape(1)
    totals = early(odd, weights, own_a, near_a, None, 0, angles, z, x, y)
    totals = early(odd, weights, own_b, near_b, totals, 1, angles, z, x, y)
    totals = add_far(1 - odd, weights, far_a, totals, angles, z, x, y)
    done, first = None, 0
    for far, planes in zip(fars, LAST_PARTS):
        done = finish(1 - odd, weights, totals, far, done, first, (angles, z, x, y))
        first += planes
    return done


def solution(mesh):
    return jax.shard_map(
        local,
        mesh=mesh,
        in_specs=(P(None, "depth", "gx", None), P("depth", "gx", None), P(), P(), P()),
        out_specs=P(None, "depth", "gx", None),
        check_vma=False,
    )
```
